32 devices in a mesh: seq: 4 (over y, x), ctx: 4 (over z), fsdp: 2 (over core).
Axes of the slice: x: 2, y: 2, z: 4, core: 2. Of those that a mesh axis runs over, the one named last changes fastest.
Arguments:
- inputs: bfloat16 [8, 512, 2048], P(('seq', 'fsdp'), 'ctx'), may hold values from -6 to 6
- block_index: int32 [8, 4, 2], P(('seq', 'fsdp'), 'ctx'), may hold values from 0 to 7, as said below
- attention_gain: float32 [2048], replicated, may hold values from 0.1 to 1.9
- query_norm_gain: float32 [128], replicated, may hold values from 0.1 to 1.9
- key_gain: float32 [128], replicated, may hold values from 0.1 to 1.9
- feedforward_gain: float32 [2048], replicated, may hold values from 0.1 to 1.9
- attention_in: bfloat16 [2048, 4096], P(('seq', 'fsdp')), may hold values from -0.125 to 0.125
- attention_out: bfloat16 [2048, 2048], P(('seq', 'fsdp')), may hold values from -0.75 to 0.75
- gate_up: bfloat16 [2048, 12288], P(('seq', 'fsdp')), may hold values from -0.125 to 0.125
- down_weight: bfloat16 [2048, 6144], P(('seq', 'fsdp')), may hold values from -0.078125 to 0.078125
- grad_output: bfloat16 [8, 512, 2048], P(('seq', 'fsdp'), 'ctx'), may hold values from -6 to 6
Outputs:
- output: bfloat16 [8, 512, 2048], P(('seq', 'fsdp'), 'ctx')
- input_grad: bfloat16 [8, 512, 2048], P(('seq', 'fsdp'), 'ctx')
- attention_gain_grad: float32 [2048], replicated
- query_gain_grad: float32 [128], replicated
- key_gain_grad: float32 [128], replicated
- feedforward_gain_grad: float32 [2048], replicated
- attention_in_grad: float32 [2048, 4096], P(('seq', 'ctx', 'fsdp'))
- attention_out_grad: float32 [2048, 2048], P(('seq', 'ctx', 'fsdp'))
- gate_up_grad: float32 [2048, 12288], P(('seq', 'ctx', 'fsdp'))
- down_grad: float32 [2048, 6144], P(('seq', 'ctx', 'fsdp'))
The draws below stay inside these ranges and needn't reach their ends.
Inputs may be any that keep to these rules, and one draw needn't show every extreme that they name: For each sequence s, block_index[s, c, 0] over c takes each of 0 to 3 once, and block_index[s, c, 1] = 7 - block_index[s, c, 0].
All inputs are finite; a program needn't handle non-finite values.
Results may differ from the reference program's by a relative error of at most 0.018.
Values may be sent and summed in bfloat16 or wider, within the bound.
No kernel may reach another device: no remote copies, remote signals or barrier semaphores. Data moves between devices by JAX's collectives and lax.ppermute only.
A program may use at most 832 MiB of HBM per device.

```python
import jax
import jax.numpy as jnp
from jax import lax

D = 2048
QUERY_HEADS = 16
KEY_VALUE_HEADS = 8
HEAD_SIZE = 128
FF = 6144
BLOCK_TOKENS = 64
PAIRS = 4
SEQ_LEN = 512
SEQS = 8
QKV = 4096


def draw_block_index(key, part):

    def ordering(subkey):
        return jax.random.permutation(subkey, PAIRS).astype(jnp.int32)
    lower = jax.vmap(ordering)(jax.random.split(key, SEQS)).astype(jnp.int32)
    upper = (2 * PAIRS - 1 - lower).astype(jnp.int32)
    return jnp.stack([lower, upper], axis=-1).astype(jnp.int32)


def shard_levels(rng, shape, shards, least, largest):
    loudness, own = 1.0, jax.random.fold_in(rng, 6)
    for axis_at, shards_of in shards:
        steps = jnp.exp(jax.random.uniform(jax.random.fold_in(own, axis_at), (shards_of,), jnp.float32, least / len(shards), largest / len(shards)))
        loudness = loudness * jnp.repeat(steps, shape[axis_at] // shards_of).reshape([-1 if axis == axis_at else 1 for axis in range(len(shape))])
    return loudness


def normal_values(rng, shape, deviation, limit, cuts=(), held_as=jnp.bfloat16):
    values = deviation * jax.random.normal(rng, shape, jnp.float32)
    if cuts:
        values = values * shard_levels(rng, shape, cuts, -0.22, 0.18)
    return jnp.clip(values, -limit, limit).astype(held_as)


def setup_inputs(seed: int = 0) -> dict:
    key_list = jax.random.split(jax.random.key(seed), 12)
    inputs = normal_values(key_list[0], (SEQS, SEQ_LEN, D), 1.0, 6.0, ((0, 8), (1, 4)))
    block_index = draw_block_index(jax.random.fold_in(key_list[11], 71), 0)
    attention_gain = jnp.clip(1.0 + 0.18 * jax.random.normal(key_list[2], (D,), jnp.float32), 0.1, 1.9)
    query_norm_gain = jnp.clip(1.0 + 0.18 * jax.random.normal(key_list[3], (HEAD_SIZE,), jnp.float32), 0.1, 1.9)
    key_gain = jnp.clip(1.0 + 0.18 * jax.random.normal(key_list[4], (HEAD_SIZE,), jnp.float32), 0.1, 1.9)
    feedforward_gain = jnp.clip(1.0 + 0.18 * jax.random.normal(key_list[5], (D,), jnp.float32), 0.1, 1.9)
    attention_in = normal_values(key_list[6], (D, QKV), D ** -0.5, 0.125, ((0, 8),))
    attention_out = normal_values(key_list[7], (D, QUERY_HEADS * HEAD_SIZE), (QUERY_HEADS * HEAD_SIZE // 32) ** -0.5, 0.75, ((0, 8),))
    gate_up = normal_values(key_list[8], (D, 2 * FF), D ** -0.5, 0.125, ((0, 8),))
    down_weight = normal_values(key_list[9], (D, FF), FF ** -0.5, 0.078125, ((0, 8),))
    grad_output = normal_values(key_list[10], (SEQS, SEQ_LEN, D), 1.0, 6.0, ((0, 8), (1, 4)))
    return {"inputs": inputs, "block_index": block_index, "attention_gain": attention_gain, "query_norm_gain": query_norm_gain, "key_gain": key_gain, "feedforward_gain": feedforward_gain, "attention_in": attention_in, "attention_out": attention_out, "gate_up": gate_up, "down_weight": down_weight, "grad_output": grad_output}


EPS = 1e-06
ROPE_BASE = 1000000.0
MASK_FLOOR = -1e+30

def rms_scale(values):
    return lax.rsqrt(lax.optimization_barrier(jnp.mean(values * values, axis=-1, keepdims=True)) + EPS)

def rms_back(grad_normed, normed_hat, scale, gain):
    grad_hat = grad_normed * gain
    inner = lax.optimization_barrier(jnp.mean(grad_hat * normed_hat, axis=-1, keepdims=True))
    return scale * (grad_hat - normed_hat * inner)

def rope_tables(token_positions):
    half = HEAD_SIZE // 2
    rates = jnp.power(jnp.float32(ROPE_BASE), jnp.arange(half, dtype=jnp.float32) * (-2.0 / HEAD_SIZE))
    angles = token_positions.astype(jnp.float32)[:, None] * rates[None, :]
    angles = jnp.concatenate([angles, angles], axis=1)
    return (jnp.cos(angles), jnp.sin(angles))

def apply_rotation(values, cosine_table, sine_table):
    half = values.shape[-1] // 2
    turned = jnp.concatenate([-values[..., half:], values[..., :half]], axis=-1)
    return values * cosine_table[:, None, :] + turned * sine_table[:, None, :]

def rotate_back(grads, cosine_table, sine_table):
    half = grads.shape[-1] // 2
    scaled = grads * sine_table[:, None, :]
    turned = jnp.concatenate([scaled[..., half:], -scaled[..., :half]], axis=-1)
    return grads * cosine_table[:, None, :] + turned

def masked_scores(query_block, query_pos, rotary_key, key_pos):
    scores = jnp.einsum('qhgd,khd->hgqk', query_block.astype(jnp.float32), rotary_key.astype(jnp.float32)) * HEAD_SIZE ** (-0.5)
    allowed = key_pos[None, :] <= query_pos[:, None]
    return (jnp.where(allowed, scores, MASK_FLOOR), allowed)

def attend(rotary_query, rotary_key, heads_value, token_positions):
    length_total = rotary_query.shape[0]
    block_list = length_total // (2 * BLOCK_TOKENS)
    head_group = QUERY_HEADS // KEY_VALUE_HEADS
    blocks_query = rotary_query.reshape(block_list, 2 * BLOCK_TOKENS, KEY_VALUE_HEADS, head_group, HEAD_SIZE)
    position_blocks = token_positions.reshape(block_list, 2 * BLOCK_TOKENS)

    def one_block(block):
        query_block, query_pos = block
        scores, allowed = masked_scores(query_block, query_pos, rotary_key, token_positions)
        peak = lax.optimization_barrier(jnp.max(scores, axis=-1))
        total = lax.optimization_barrier(jnp.sum(jnp.where(allowed, jnp.exp(scores - peak[..., None]), 0.0), axis=-1))
        total_logarithm = peak + jnp.log(total)
        weights = jnp.where(allowed, jnp.exp(scores - total_logarithm[..., None]), 0.0).astype(jnp.bfloat16)
        attended_rows = jnp.einsum('hgqk,khd->qhgd', weights.astype(jnp.float32), heads_value.astype(jnp.float32))
        return (attended_rows.astype(jnp.bfloat16), total_logarithm)
    attended_rows, total_logarithm = lax.map(one_block, (blocks_query, position_blocks))
    return (attended_rows.reshape(length_total, KEY_VALUE_HEADS, head_group, HEAD_SIZE), total_logarithm)

def attention_backward(rotary_query, rotary_key, heads_value, token_positions, attended_rows, total_logarithm, attended_gradient):
    length_total = rotary_query.shape[0]
    block_list = length_total // (2 * BLOCK_TOKENS)
    head_group = QUERY_HEADS // KEY_VALUE_HEADS
    scale = HEAD_SIZE ** (-0.5)
    delta_rows = lax.optimization_barrier(jnp.sum(attended_gradient.astype(jnp.float32) * attended_rows.astype(jnp.float32), axis=-1))
    blocks_delta = jnp.transpose(delta_rows.reshape(block_list, 2 * BLOCK_TOKENS, KEY_VALUE_HEADS, head_group), (0, 2, 3, 1))
    blocks_query = rotary_query.reshape(block_list, 2 * BLOCK_TOKENS, KEY_VALUE_HEADS, head_group, HEAD_SIZE)
    block_gradients = attended_gradient.reshape(block_list, 2 * BLOCK_TOKENS, KEY_VALUE_HEADS, head_group, HEAD_SIZE)
    position_blocks = token_positions.reshape(block_list, 2 * BLOCK_TOKENS)

    def one_block(carry, block):
        key_grads, value_grads = carry
        query_block, query_pos, grad_block, delta_block, log_block = block
        scores, allowed = masked_scores(query_block, query_pos, rotary_key, token_positions)
        probs = jnp.where(allowed, jnp.exp(scores - log_block[..., None]), 0.0)
        weights = probs.astype(jnp.bfloat16)
        grad_probs = jnp.einsum('qhgd,khd->hgqk', grad_block.astype(jnp.float32), heads_value.astype(jnp.float32))
        grad_scores = (probs * (grad_probs - delta_block[..., None])).astype(jnp.bfloat16)
        grad_query = jnp.einsum('hgqk,khd->qhgd', grad_scores.astype(jnp.float32), rotary_key.astype(jnp.float32)) * scale
        key_grads = key_grads + jnp.einsum('hgqk,qhgd->khd', grad_scores.astype(jnp.float32), query_block.astype(jnp.float32))
        value_grads = value_grads + jnp.einsum('hgqk,qhgd->khd', weights.astype(jnp.float32), grad_block.astype(jnp.float32))
        return ((key_grads, value_grads), grad_query)
    zero_fill = jnp.zeros((length_total, KEY_VALUE_HEADS, HEAD_SIZE), jnp.float32)
    carry, grad_query = lax.scan(one_block, (zero_fill, zero_fill), (blocks_query, position_blocks, block_gradients, blocks_delta, total_logarithm))
    return (grad_query.reshape(length_total, QUERY_HEADS, HEAD_SIZE), carry[0] * scale, carry[1])

def layer(rows_in, index_row, grad_rows, attention_gain, query_norm_gain, key_gain, feedforward_gain, attention_in, attention_out, gate_up, down_weight):
    length_total = rows_in.shape[0]
    head_group = QUERY_HEADS // KEY_VALUE_HEADS
    query_width = QUERY_HEADS * HEAD_SIZE
    key_width = KEY_VALUE_HEADS * HEAD_SIZE
    token_positions = (index_row[:, :, None] * BLOCK_TOKENS + jnp.arange(BLOCK_TOKENS, dtype=jnp.int32)[None, None, :]).reshape(-1).astype(jnp.int32)
    rows = rows_in.astype(jnp.float32)
    first_scale = rms_scale(rows)
    first_hat = rows * first_scale
    first_normed = (first_hat * attention_gain).astype(jnp.bfloat16)
    projected_rows = jnp.dot(first_normed, attention_in, preferred_element_type=jnp.float32)
    query = projected_rows[:, :query_width].reshape(length_total, QUERY_HEADS, HEAD_SIZE)
    key_rows_all = projected_rows[:, query_width:query_width + key_width].reshape(length_total, KEY_VALUE_HEADS, HEAD_SIZE)
    heads_value = projected_rows[:, query_width + key_width:].astype(jnp.bfloat16).reshape(length_total, KEY_VALUE_HEADS, HEAD_SIZE)
    query_scale = rms_scale(query)
    query_normalized = query * query_scale
    key_scale = rms_scale(key_rows_all)
    key_hat = key_rows_all * key_scale
    cosine_table, sine_table = rope_tables(token_positions)
    rotary_query = apply_rotation(query_normalized * query_norm_gain, cosine_table, sine_table).astype(jnp.bfloat16).reshape(length_total, KEY_VALUE_HEADS, head_group, HEAD_SIZE)
    rotary_key = apply_rotation(key_hat * key_gain, cosine_table, sine_table).astype(jnp.bfloat16)
    attended_rows, total_logarithm = attend(rotary_query, rotary_key, heads_value, token_positions)
    attended_flat = attended_rows.reshape(length_total, query_width)
    middle = rows + jnp.dot(attended_flat, attention_out.T, preferred_element_type=jnp.float32)
    second_scale = rms_scale(middle)
    second_hat = middle * second_scale
    second_normed = (second_hat * feedforward_gain).astype(jnp.bfloat16)
    gate_values = jnp.dot(second_normed, gate_up, preferred_element_type=jnp.float32)
    gate = gate_values[:, :FF]
    upward = gate_values[:, FF:]
    hidden = (jax.nn.silu(gate) * upward).astype(jnp.bfloat16)
    result = middle + jnp.dot(hidden, down_weight.T, preferred_element_type=jnp.float32)
    output = result.astype(jnp.bfloat16)
    grad_hidden = jnp.dot(grad_rows, down_weight, preferred_element_type=jnp.float32)
    sigmoid_gate = jax.nn.sigmoid(gate)
    grad_gate = grad_hidden * upward * sigmoid_gate * (1.0 + gate * (1.0 - sigmoid_gate))
    grad_upward = grad_hidden * jax.nn.silu(gate)
    grad_gate_up = jnp.concatenate([grad_gate, grad_upward], axis=1).astype(jnp.bfloat16)
    grad_second = jnp.dot(grad_gate_up, gate_up.T, preferred_element_type=jnp.float32)
    feedforward_part = lax.optimization_barrier(jnp.sum(grad_second * second_hat, axis=0))
    grad_middle = grad_rows.astype(jnp.float32) + rms_back(grad_second, second_hat, second_scale, feedforward_gain)
    grad_middle_short = grad_middle.astype(jnp.bfloat16)
    attended_gradient = jnp.dot(grad_middle_short, attention_out, preferred_element_type=jnp.float32).astype(jnp.bfloat16)
    rotary_query_gradient, rotary_key_gradient, value_gradient = attention_backward(rotary_query, rotary_key, heads_value, token_positions, attended_rows, total_logarithm, attended_gradient.reshape(length_total, KEY_VALUE_HEADS, head_group, HEAD_SIZE))
    unrotated_query = rotate_back(rotary_query_gradient, cosine_table, sine_table)
    unrotated_key = rotate_back(rotary_key_gradient, cosine_table, sine_table)
    query_part = lax.optimization_barrier(jnp.sum(unrotated_query * query_normalized, axis=(0, 1)))
    key_portion = lax.optimization_barrier(jnp.sum(unrotated_key * key_hat, axis=(0, 1)))
    grad_query = rms_back(unrotated_query, query_normalized, query_scale, query_norm_gain)
    grad_key = rms_back(unrotated_key, key_hat, key_scale, key_gain)
    grad_projected = jnp.concatenate([grad_query.reshape(length_total, query_width), grad_key.reshape(length_total, key_width), value_gradient.reshape(length_total, key_width)], axis=1).astype(jnp.bfloat16)
    grad_first = jnp.dot(grad_projected, attention_in.T, preferred_element_type=jnp.float32)
    attention_part = lax.optimization_barrier(jnp.sum(grad_first * first_hat, axis=0))
    input_grad = (grad_middle + rms_back(grad_first, first_hat, first_scale, attention_gain)).astype(jnp.bfloat16)
    parts = (attention_part, query_part, key_portion, feedforward_part, jnp.dot(first_normed.T, grad_projected, preferred_element_type=jnp.float32), jnp.dot(grad_middle_short.T, attended_flat, preferred_element_type=jnp.float32), jnp.dot(second_normed.T, grad_gate_up, preferred_element_type=jnp.float32), jnp.dot(grad_rows.T, hidden, preferred_element_type=jnp.float32))
    return (output, input_grad, parts)

def reference(inputs, block_index, attention_gain, query_norm_gain, key_gain, feedforward_gain, attention_in, attention_out, gate_up, down_weight, grad_output):

    def one_sequence(carry, sequence):
        rows_in, index_row, grad_rows = sequence
        output_row, input_grad_row, parts = layer(rows_in, index_row, grad_rows, attention_gain, query_norm_gain, key_gain, feedforward_gain, attention_in, attention_out, gate_up, down_weight)
        return (jax.tree.map(jnp.add, carry, parts), (output_row, input_grad_row))
    start_state = (jnp.zeros((D,), jnp.float32), jnp.zeros((HEAD_SIZE,), jnp.float32), jnp.zeros((HEAD_SIZE,), jnp.float32), jnp.zeros((D,), jnp.float32), jnp.zeros(attention_in.shape, jnp.float32), jnp.zeros(attention_out.shape, jnp.float32), jnp.zeros(gate_up.shape, jnp.float32), jnp.zeros(down_weight.shape, jnp.float32))
    sums, outcome = lax.scan(one_sequence, start_state, (inputs, block_index, grad_output))
    return (outcome[0], outcome[1], sums[0], sums[1], sums[2], sums[3], sums[4], sums[5], sums[6], sums[7])
```

```python
import jax
import jax.numpy as jnp
from jax import lax
from jax.sharding import PartitionSpec as P

D = 2048
QUERY_HEADS = 16
KEY_VALUE_HEADS = 8
HEAD_SIZE = 128
FF = 6144

EPS = 1e-06
ROPE_BASE = 1000000.0
MASK_FLOOR = -1e30
PLANE = ("seq", "fsdp")
F32 = jnp.float32
BF16 = jnp.bfloat16


def rms_scale(values):
    return lax.rsqrt(jnp.mean(values * values, axis=-1, keepdims=True) + EPS)


def rms_back(grad_normed, normed_hat, scale, gain):
    grad_hat = grad_normed * gain
    inner = jnp.mean(grad_hat * normed_hat, axis=-1, keepdims=True)
    return scale * (grad_hat - normed_hat * inner)


def rope_tables(token_positions):
    half = HEAD_SIZE // 2
    rates = jnp.power(F32(ROPE_BASE), jnp.arange(half, dtype=F32) * (-2.0 / HEAD_SIZE))
    angles = token_positions.astype(F32)[:, None] * rates[None, :]
    angles = jnp.concatenate([angles, angles], axis=1)
    return (jnp.cos(angles), jnp.sin(angles))


def apply_rotation(values, cosine_table, sine_table):
    half = values.shape[-1] // 2
    turned = jnp.concatenate([-values[..., half:], values[..., :half]], axis=-1)
    return values * cosine_table[:, None, :] + turned * sine_table[:, None, :]


def rotate_back(grads, cosine_table, sine_table):
    half = grads.shape[-1] // 2
    scaled = grads * sine_table[:, None, :]
    turned = jnp.concatenate([scaled[..., half:], -scaled[..., :half]], axis=-1)
    return grads * cosine_table[:, None, :] + turned


def rows_by(left, right):
    return jnp.dot(left, right, preferred_element_type=F32)


def rows_by_t(left, right):
    return lax.dot_general(left, right, (((1,), (1,)), ((), ())), preferred_element_type=F32)


def t_by_rows(left, right):
    return lax.dot_general(left, right, (((0,), (0,)), ((), ())), preferred_element_type=F32)


def gather_ctx(rows):
    return lax.all_gather(rows, "ctx", axis=0, tiled=True)


def gather_plane(rows):
    return lax.all_gather(rows, PLANE, axis=0, tiled=True)


def scatter_ctx(partials):
    parts = lax.axis_size("ctx")
    pieces = lax.all_to_all(partials.astype(BF16), "ctx", 0, 0, tiled=True)
    pieces = pieces.reshape(parts, partials.shape[0] // parts, partials.shape[1])
    return jnp.sum(pieces.astype(F32), axis=0)


def scatter_weight(grad):
    seqs, ctxs, cores = lax.axis_size("seq"), lax.axis_size("ctx"), lax.axis_size("fsdp")
    rows = grad.shape[0] // (seqs * ctxs * cores)
    grad = grad.astype(BF16).reshape(seqs, ctxs, cores, rows, grad.shape[1])
    grad = jnp.transpose(grad, (0, 2, 1, 3, 4)).reshape(-1, grad.shape[-1])
    grad = lax.psum_scatter(grad, PLANE, scatter_dimension=0, tiled=True)
    grad = lax.all_to_all(grad, "ctx", 0, 0, tiled=True)
    return grad.reshape(ctxs, rows, grad.shape[-1])


def join_columns(pieces):
    parts, rows, width = pieces.shape
    return jnp.transpose(pieces, (1, 0, 2)).reshape(rows, parts * width).astype(F32)


def local(
    inputs,
    block_index,
    attention_gain,
    query_norm_gain,
    key_gain,
    feedforward_gain,
    attention_in,
    attention_out,
    gate_up,
    down_weight,
    grad_output,
):
    parts = lax.axis_size("ctx")
    me = lax.axis_index("ctx")
    tokens = inputs.shape[1]
    half_rows = tokens // 2
    length = tokens * parts
    query_heads = QUERY_HEADS // parts
    key_heads = max(1, KEY_VALUE_HEADS // parts)
    copies = key_heads * parts // KEY_VALUE_HEADS
    group = query_heads // key_heads
    query_width = query_heads * HEAD_SIZE
    key_width = key_heads * HEAD_SIZE
    all_query = QUERY_HEADS * HEAD_SIZE
    all_key = KEY_VALUE_HEADS * HEAD_SIZE
    hidden_width = FF // parts
    scale = HEAD_SIZE ** (-0.5)

    def columns(weight, start, width):
        return lax.dynamic_slice_in_dim(weight, start, width, axis=1)

    key_start = (me // copies) * key_width
    weight_in = gather_plane(
        jnp.concatenate(
            [
                columns(attention_in, me * query_width, query_width),
                columns(attention_in, all_query + key_start, key_width),
                columns(attention_in, all_query + all_key + key_start, key_width),
            ],
            axis=1,
        )
    )
    own_inputs = inputs[0]
    sequence_inputs = gather_ctx(own_inputs)
    blocks = lax.all_gather(block_index[0, 0], "ctx", axis=0, tiled=True)
    weight_out = gather_plane(attention_out)
    weight_gate_up = gather_plane(
        jnp.concatenate(
            [
                columns(gate_up, me * hidden_width, hidden_width),
                columns(gate_up, FF + me * hidden_width, hidden_width),
            ],
            axis=1,
        )
    )
    weight_down = gather_plane(columns(down_weight, me * hidden_width, hidden_width))
    own_grad = grad_output[0]
    sequence_grad = gather_ctx(own_grad)

    steps_along = jnp.arange(half_rows, dtype=jnp.int32)
    positions = (blocks[:, None] * half_rows + steps_along[None, :]).reshape(-1)
    cosine_table, sine_table = rope_tables(positions)

    rows = sequence_inputs.astype(F32)
    first_scale = rms_scale(rows)
    first_hat = rows * first_scale
    first_normed = (first_hat * attention_gain).astype(BF16)
    projected = rows_by(first_normed, weight_in)
    query = projected[:, :query_width].reshape(length, query_heads, HEAD_SIZE)
    key = projected[:, query_width : query_width + key_width].reshape(length, key_heads, HEAD_SIZE)
    value = projected[:, query_width + key_width :].astype(BF16)
    value = value.reshape(length, key_heads, HEAD_SIZE)
    query_scale = rms_scale(query)
    query_hat = query * query_scale
    key_scale = rms_scale(key)
    key_hat = key * key_scale
    rotary_query = (
        apply_rotation(query_hat * query_norm_gain, cosine_table, sine_table)
        .astype(BF16)
        .reshape(length, key_heads, group, HEAD_SIZE)
    )
    rotary_key = apply_rotation(key_hat * key_gain, cosine_table, sine_table).astype(BF16)

    scores = (
        jnp.einsum("qhgd,khd->hgqk", rotary_query, rotary_key, preferred_element_type=F32) * scale
    )
    allowed = positions[None, :] <= positions[:, None]
    scores = jnp.where(allowed, scores, MASK_FLOOR)
    peak = jnp.max(scores, axis=-1, keepdims=True)
    total = jnp.sum(jnp.where(allowed, jnp.exp(scores - peak), 0.0), axis=-1, keepdims=True)
    total_logarithm = peak + jnp.log(total)
    probs = jnp.where(allowed, jnp.exp(scores - total_logarithm), 0.0)
    weights = probs.astype(BF16)
    attended = jnp.einsum("hgqk,khd->qhgd", weights, value, preferred_element_type=F32)
    attended = attended.astype(BF16).reshape(length, query_width)

    own_attended = lax.all_to_all(attended, "ctx", 0, 1, tiled=True)
    own_rows = own_inputs.astype(F32)
    middle = own_rows + rows_by_t(own_attended, weight_out)
    second_scale = rms_scale(middle)
    second_hat = middle * second_scale
    second_normed = (second_hat * feedforward_gain).astype(BF16)
    sequence_second = gather_ctx(second_normed)

    grad_hidden = rows_by(sequence_grad, weight_down)
    gate_values = rows_by(sequence_second, weight_gate_up)
    gate = gate_values[:, :hidden_width]
    upward = gate_values[:, hidden_width:]
    sigmoid_gate = jax.nn.sigmoid(gate)
    silu_gate = gate * sigmoid_gate
    hidden = (silu_gate * upward).astype(BF16)
    grad_gate = grad_hidden * upward * sigmoid_gate * (1.0 + gate * (1.0 - sigmoid_gate))
    grad_upward = grad_hidden * silu_gate
    grad_gate_up = jnp.concatenate([grad_gate, grad_upward], axis=1).astype(BF16)
    grad_second = scatter_ctx(rows_by_t(grad_gate_up, weight_gate_up))

    down_pieces = scatter_weight(t_by_rows(sequence_grad, hidden))
    gate_up_pieces = scatter_weight(t_by_rows(sequence_second, grad_gate_up))
    output = middle + scatter_ctx(rows_by_t(hidden, weight_down))

    feedforward_part = jnp.sum(grad_second * second_hat, axis=0)
    grad_middle = own_grad.astype(F32) + rms_back(
        grad_second, second_hat, second_scale, feedforward_gain
    )
    grad_middle_short = grad_middle.astype(BF16)
    own_attended_grad = rows_by(grad_middle_short, weight_out).astype(BF16)
    attended_grad = lax.all_to_all(own_attended_grad, "ctx", 1, 0, tiled=True)
    sequence_middle_grad = gather_ctx(grad_middle_short)
    out_pieces = scatter_weight(t_by_rows(sequence_middle_grad, attended))

    delta = jnp.sum(
        (attended_grad.astype(F32) * attended.astype(F32)).reshape(
            length, key_heads, group, HEAD_SIZE
        ),
        axis=-1,
    )
    head_grads = attended_grad.reshape(length, key_heads, group, HEAD_SIZE)
    grad_probs = jnp.einsum("qhgd,khd->hgqk", head_grads, value, preferred_element_type=F32)
    grad_scores = (probs * (grad_probs - jnp.transpose(delta, (1, 2, 0))[..., None])).astype(BF16)
    grad_rotary_query = (
        jnp.einsum("hgqk,khd->qhgd", grad_scores, rotary_key, preferred_element_type=F32) * scale
    )
    grad_rotary_key = (
        jnp.einsum("hgqk,qhgd->khd", grad_scores, rotary_query, preferred_element_type=F32) * scale
    )
    value_grad = jnp.einsum("hgqk,qhgd->khd", weights, head_grads, preferred_element_type=F32)
    unrotated_query = rotate_back(
        grad_rotary_query.reshape(length, query_heads, HEAD_SIZE), cosine_table, sine_table
    )
    unrotated_key = rotate_back(grad_rotary_key, cosine_table, sine_table)
    query_part = jnp.sum(unrotated_query * query_hat, axis=(0, 1))
    key_part = jnp.sum(unrotated_key * key_hat, axis=(0, 1))
    grad_query = rms_back(unrotated_query, query_hat, query_scale, query_norm_gain)
    grad_key = rms_back(unrotated_key, key_hat, key_scale, key_gain)
    grad_projected = jnp.concatenate(
        [
            grad_query.reshape(length, query_width),
            grad_key.reshape(length, key_width),
            value_grad.reshape(length, key_width),
        ],
        axis=1,
    ).astype(BF16)
    partial_first = rows_by_t(grad_projected, weight_in)
    attention_part = jnp.sum(partial_first * first_hat, axis=0)
    grad_first = scatter_ctx(partial_first)
    in_pieces = scatter_weight(t_by_rows(first_normed, grad_projected))
    own_scale = rms_scale(own_rows)
    input_grad = grad_middle + rms_back(
        grad_first, own_rows * own_scale, own_scale, attention_gain
    )
    gain_sums = lax.psum(
        (attention_part, query_part, key_part, feedforward_part), ("seq", "ctx", "fsdp")
    )

    def merge_copies(pieces):
        shape = pieces.shape
        return jnp.sum(pieces.reshape(shape[0] // copies, copies, shape[1], shape[2]), axis=1)

    attention_in_grad = jnp.concatenate(
        [
            join_columns(in_pieces[:, :, :query_width]),
            join_columns(
                merge_copies(in_pieces[:, :, query_width : query_width + key_width].astype(F32))
            ),
            join_columns(merge_copies(in_pieces[:, :, query_width + key_width :].astype(F32))),
        ],
        axis=1,
    )
    gate_up_grad = jnp.concatenate(
        [
            join_columns(gate_up_pieces[:, :, :hidden_width]),
            join_columns(gate_up_pieces[:, :, hidden_width:]),
        ],
        axis=1,
    )
    return (
        output.astype(BF16)[None],
        input_grad.astype(BF16)[None],
        gain_sums[0],
        gain_sums[1],
        gain_sums[2],
        gain_sums[3],
        attention_in_grad,
        join_columns(out_pieces),
        gate_up_grad,
        join_columns(down_pieces),
    )


def solution(mesh):
    tokens = P(("seq", "fsdp"), "ctx", None)
    weight = P(("seq", "fsdp"), None)
    grad = P(("seq", "ctx", "fsdp"), None)
    in_specs = (tokens, tokens, P(), P(), P(), P(), weight, weight, weight, weight, tokens)
    out_specs = (tokens, tokens, P(), P(), P(), P(), grad, grad, grad, grad)
    return jax.shard_map(local, mesh=mesh, in_specs=in_specs, out_specs=out_specs, check_vma=False)
```

```python
import jax
import jax.numpy as jnp
from jax import lax
from jax.experimental import pallas as pl
from jax.experimental.pallas import tpu as pltpu
from jax.sharding import PartitionSpec as P


D = 2048
QUERY_HEADS = 16
KEY_VALUE_HEADS = 8
HEAD_SIZE = 128
FF = 6144

EPS = 1e-06
ROPE_BASE = 1000000.0
MASK_FLOOR = -1e30
PLANE = ("seq", "fsdp")
F32 = jnp.float32
BF16 = jnp.bfloat16


def rms_scale(values):
    return lax.rsqrt(jnp.mean(values * values, axis=-1, keepdims=True) + EPS)


def rms_back(grad_normed, normed_hat, scale, gain):
    grad_hat = grad_normed * gain
    inner = jnp.mean(grad_hat * normed_hat, axis=-1, keepdims=True)
    return scale * (grad_hat - normed_hat * inner)


def rope_tables(token_positions):
    half = HEAD_SIZE // 2
    rates = jnp.power(F32(ROPE_BASE), jnp.arange(half, dtype=F32) * (-2.0 / HEAD_SIZE))
    angles = token_positions.astype(F32)[:, None] * rates[None, :]
    cosine, sine = jnp.cos(angles), jnp.sin(angles)
    return (
        jnp.concatenate([cosine, cosine], axis=1),
        jnp.concatenate([-sine, sine], axis=1),
    )


def turn(values):
    return pltpu.roll(values, HEAD_SIZE // 2, 1)


def rows_by(left, right):
    return jnp.dot(left, right, preferred_element_type=F32)


def rows_by_t(left, right):
    return lax.dot_general(left, right, (((1,), (1,)), ((), ())), preferred_element_type=F32)


def t_by_rows(left, right):
    return lax.dot_general(left, right, (((0,), (0,)), ((), ())), preferred_element_type=F32)


def swap(values, axis, step):
    return lax.ppermute(values, axis, [(i, i ^ step) for i in range(lax.axis_size(axis))])


def gather_ctx(rows):
    parts = lax.axis_size("ctx")
    return jnp.concatenate([rows] + [swap(rows, "ctx", k) for k in range(1, parts)], axis=0)


def gather_plane(rows):
    return lax.all_gather(rows, PLANE, axis=0, tiled=True)


def pick_kernel(picks, starts, *refs):
    sources, out, sems = refs[:-2], refs[-2], refs[-1]
    copies, at = [], 0
    for n, (source, width) in enumerate(picks):
        start = pl.multiple_of(starts[n], HEAD_SIZE)
        copies.append(
            pltpu.make_async_copy(
                sources[source].at[:, pl.ds(start, width)],
                out.at[:, pl.ds(at, width)],
                sems.at[n],
            )
        )
        at += width
    for copy in copies:
        copy.start()
    for copy in copies:
        copy.wait()


def pick_columns(sources, picks):
    rows = sources[0].shape[0]
    starts = jnp.stack([jnp.asarray(start, jnp.int32) for _, start, _ in picks])
    anywhere = pl.BlockSpec(memory_space=pl.ANY)
    return pl.pallas_call(
        lambda *refs: pick_kernel([(source, width) for source, _, width in picks], *refs),
        out_shape=jax.ShapeDtypeStruct((rows, sum(width for _, _, width in picks)), BF16),
        in_specs=[pl.BlockSpec(memory_space=pltpu.SMEM)] + [anywhere] * len(sources),
        out_specs=pl.BlockSpec(memory_space=pltpu.VMEM),
        scratch_shapes=[pltpu.SemaphoreType.DMA((len(picks),))],
        name="pick_columns",
    )(starts, *sources)


def scatter_ctx(partials):
    parts = lax.axis_size("ctx")
    tokens = partials.shape[0] // parts
    pieces = [
        swap(partials[k * tokens : (k + 1) * tokens].astype(BF16), "ctx", k)
        for k in range(1, parts)
    ]
    total = partials[:tokens]
    for piece in pieces:
        total = total + piece.astype(F32)
    return total


def gather_heads(attended):
    parts = lax.axis_size("ctx")
    tokens = attended.shape[0] // parts
    pieces = [attended] + [swap(attended, "ctx", j) for j in range(1, parts)]
    whole = pl.BlockSpec(memory_space=pltpu.VMEM)
    return pl.pallas_call(
        lambda *refs: join_heads_kernel(tokens, *refs),
        out_shape=jax.ShapeDtypeStruct((parts * tokens, parts * attended.shape[1]), BF16),
        in_specs=[whole] * parts,
        out_specs=whole,
        name="join_heads",
    )(*pieces)


def join_heads_kernel(tokens, *refs):
    pieces, out = refs[:-1], refs[-1]
    width = pieces[0].shape[1]
    for j, piece in enumerate(pieces):
        for k in range(len(pieces)):
            at = (k ^ j) * tokens
            out[k * tokens : (k + 1) * tokens, j * width : (j + 1) * width] = piece[
                at : at + tokens, :
            ]


def tokens_to_heads(rows):
    parts = lax.axis_size("ctx")
    width = rows.shape[1] // parts
    pieces = [rows[:, :width]]
    for k in range(1, parts):
        pieces.append(swap(rows[:, k * width : (k + 1) * width], "ctx", k))
    return jnp.concatenate(pieces, axis=0)


def tokens_to_rows(rows):
    seqs, ctxs = lax.axis_size("seq"), lax.axis_size("ctx")
    me = lax.axis_index("ctx")
    width = rows.shape[1] // (seqs * ctxs)
    pieces = []
    for k in range(ctxs):
        blocks = [
            lax.dynamic_slice_in_dim(rows, (s * ctxs + (me ^ k)) * width, width, axis=1)
            for s in range(seqs)
        ]
        piece = jnp.concatenate(blocks, axis=1)
        pieces.append(piece if k == 0 else swap(piece, "ctx", k))
    return jnp.concatenate(pieces, axis=0)


def scatter_plane(grad):
    return lax.psum_scatter(grad, PLANE, scatter_dimension=0, tiled=True)


def scatter_plane_swaps(grad):
    seqs, cores = lax.axis_size("seq"), lax.axis_size("fsdp")
    seq, core = lax.axis_index("seq"), lax.axis_index("fsdp")
    rows = grad.shape[0] // (seqs * cores)
    grad = grad.reshape(seqs, cores, rows, grad.shape[1])

    def of_core(k):
        return lax.dynamic_slice_in_dim(grad, core ^ k, 1, axis=1)[:, 0]

    total = of_core(0).astype(F32)
    for k in range(1, cores):
        other = swap(of_core(k), "fsdp", k)
        total = total + other.astype(F32)
    out = lax.dynamic_slice_in_dim(total, seq, 1, axis=0)[0]
    short = total.astype(BF16)
    for k in range(1, seqs):
        piece = lax.dynamic_slice_in_dim(short, seq ^ k, 1, axis=0)[0]
        other = swap(piece, "seq", k)
        out = out + other.astype(F32)
    return out.astype(BF16)


def scatter_weight(grad, over_plane):
    ctxs, cores = lax.axis_size("ctx"), lax.axis_size("fsdp")
    ctx = lax.axis_index("ctx")
    grad = over_plane(grad)
    rows = grad.shape[0] // ctxs
    pieces = []
    for k in range(ctxs):
        piece = lax.dynamic_slice_in_dim(grad, (ctx ^ k) * rows, rows, axis=0)
        pairs = [
            (c * cores + f, f * ctxs + (c ^ k)) for c in range(ctxs) for f in range(cores)
        ]
        pieces.append(lax.ppermute(piece, ("ctx", "fsdp"), pairs))
    return pieces


def sum_everywhere(values):
    for axis in ("ctx", "seq", "fsdp"):
        size = lax.axis_size(axis)
        sums = [values] + [swap(values, axis, k) for k in range(1, size)]
        while len(sums) > 1:
            sums = [sums[i] + sums[i + 1] for i in range(0, len(sums), 2)]
        values = sums[0]
    return values


def join_kernel(segments, source_ref, *refs):
    pieces, outs = refs[: -len(segments)], refs[-len(segments) :]
    for out, group in zip(outs, segments):
        if any(copies > 1 for _, _, _, copies in group):
            out[...] = jnp.zeros_like(out)
    for k, piece in enumerate(pieces):
        owner = source_ref[0] ^ k
        for out, group in zip(outs, segments):
            for start, width, base, copies in group:
                at = pl.multiple_of(base + (owner // copies) * width, HEAD_SIZE)
                values = piece[:, start : start + width].astype(F32)
                if copies > 1:
                    values = values + out[:, pl.ds(at, width)]
                out[:, pl.ds(at, width)] = values


def join_pieces(source, pieces, segments):
    rows = pieces[0].shape[0]
    widths = [
        sum(width * len(pieces) // copies for _, width, _, copies in group) for group in segments
    ]
    whole = pl.BlockSpec(memory_space=pltpu.VMEM)
    return pl.pallas_call(
        lambda *refs: join_kernel(segments, *refs),
        out_shape=[jax.ShapeDtypeStruct((rows, width), F32) for width in widths],
        in_specs=[pl.BlockSpec(memory_space=pltpu.SMEM)] + [whole] * len(pieces),
        out_specs=[whole] * len(segments),
        name="join_pieces",
    )(source.astype(jnp.int32)[None], *pieces)


def head_columns(ref, head):
    return ref[:, head * HEAD_SIZE : (head + 1) * HEAD_SIZE]


def normalized(values):
    scale = lax.rsqrt(jnp.mean(values * values, axis=-1, keepdims=True) + EPS)
    return values * scale, scale


def rotated(normed, cosine, sine):
    return (normed * cosine + turn(normed) * sine).astype(BF16)


def row_blocks(length):
    step = min(length, 512)
    return [(at, step) for at in range(0, length, step)]


def forward_kernel(query_heads, key_heads, *refs):
    (projected, cosine_ref, sine_ref, column, row, query_gain, key_gain, attended, logs) = refs
    cosine, sine = cosine_ref[...], sine_ref[...]
    group = query_heads // key_heads
    scale = HEAD_SIZE ** (-0.5)
    length = projected.shape[0]
    for key_head in range(key_heads):
        key_hat, _ = normalized(head_columns(projected, query_heads + key_head))
        key = rotated(key_hat * key_gain[...], cosine, sine)
        value = head_columns(projected, query_heads + key_heads + key_head).astype(BF16)
        for head in range(key_head * group, (key_head + 1) * group):
            query_hat, _ = normalized(head_columns(projected, head))
            query = rotated(query_hat * query_gain[...], cosine, sine)
            for at, step in row_blocks(length):
                scores = rows_by_t(query[at : at + step], key) * scale
                allowed = row[...] <= column[at : at + step, :]
                scores = jnp.where(allowed, scores, MASK_FLOOR)
                peak = jnp.max(scores, axis=-1, keepdims=True)
                total = jnp.sum(jnp.exp(scores - peak), axis=-1, keepdims=True)
                log_total = peak + jnp.log(total)
                weights = jnp.exp(scores - log_total).astype(BF16)
                attended[at : at + step, head * HEAD_SIZE : (head + 1) * HEAD_SIZE] = rows_by(
                    weights, value
                ).astype(BF16)
                logs[at : at + step, head : head + 1] = log_total


def backward_kernel(query_heads, key_heads, *refs):
    (
        projected,
        cosine_ref,
        sine_ref,
        column,
        row,
        query_gain,
        key_gain,
        logs,
        attended,
        attended_grad,
        grad_projected,
        gain_parts,
    ) = refs
    cosine, sine = cosine_ref[...], sine_ref[...]
    group = query_heads // key_heads
    scale = HEAD_SIZE ** (-0.5)
    length = projected.shape[0]
    query_part = jnp.zeros((1, HEAD_SIZE), F32)
    key_part = jnp.zeros((1, HEAD_SIZE), F32)

    def finish(grad_rotary, hat, factor, gain):
        grad = grad_rotary * scale
        unrotated = grad * cosine - turn(grad) * sine
        part = jnp.sum(unrotated * hat, axis=0, keepdims=True)
        grad_hat = unrotated * gain
        inner = jnp.mean(grad_hat * hat, axis=-1, keepdims=True)
        return (factor * (grad_hat - hat * inner)).astype(BF16), part

    def store(head, values):
        grad_projected[:, head * HEAD_SIZE : (head + 1) * HEAD_SIZE] = values

    for key_head in range(key_heads):
        key_hat, key_scale = normalized(head_columns(projected, query_heads + key_head))
        key = rotated(key_hat * key_gain[...], cosine, sine)
        value = head_columns(projected, query_heads + key_heads + key_head).astype(BF16)
        key_acc = jnp.zeros((length, HEAD_SIZE), F32)
        value_acc = jnp.zeros((length, HEAD_SIZE), F32)
        for head in range(key_head * group, (key_head + 1) * group):
            query_hat, query_scale = normalized(head_columns(projected, head))
            query = rotated(query_hat * query_gain[...], cosine, sine)
            grad = head_columns(attended_grad, head)
            delta = jnp.sum(
                grad.astype(F32) * head_columns(attended, head).astype(F32), axis=-1, keepdims=True
            )
            query_accs = []
            for at, step in row_blocks(length):
                rows = slice(at, at + step)
                scores = rows_by_t(query[rows], key) * scale
                allowed = row[...] <= column[rows, :]
                scores = jnp.where(allowed, scores, MASK_FLOOR)
                probs = jnp.exp(scores - logs[rows, head : head + 1])
                grad_probs = rows_by_t(grad[rows], value)
                grad_scores = (probs * (grad_probs - delta[rows])).astype(BF16)
                query_accs.append(rows_by(grad_scores, key))
                key_acc = key_acc + t_by_rows(grad_scores, query[rows])
                value_acc = value_acc + t_by_rows(probs.astype(BF16), grad[rows])
            query_acc = jnp.concatenate(query_accs, axis=0)
            grads, part = finish(query_acc, query_hat, query_scale, query_gain[...])
            query_part = query_part + part
            store(head, grads)
        grads, part = finish(key_acc, key_hat, key_scale, key_gain[...])
        key_part = key_part + part
        store(query_heads + key_head, grads)
        store(query_heads + key_heads + key_head, value_acc.astype(BF16))
    gain_parts[0:1, :] = query_part
    gain_parts[1:2, :] = key_part


def attention_call(kernel, heads, operands, outs):
    whole = pl.BlockSpec(memory_space=pltpu.VMEM)
    return pl.pallas_call(
        lambda *refs: kernel(*heads, *refs),
        out_shape=outs,
        in_specs=[whole] * len(operands),
        out_specs=[whole] * len(outs),
    )(*operands)


def weight_grad_kernel(left, right, out, turned):
    @pl.when(pl.program_id(0) == 0)
    def _():
        turned[...] = left[...].T

    out[...] = rows_by(turned[...], right[...]).astype(BF16)


def weight_grad(left, right):
    length, depth = left.shape
    width = right.shape[1]
    tile = HEAD_SIZE * 4 if width % (HEAD_SIZE * 4) == 0 else HEAD_SIZE
    return pl.pallas_call(
        weight_grad_kernel,
        grid=(width // tile,),
        out_shape=jax.ShapeDtypeStruct((depth, width), BF16),
        in_specs=[
            pl.BlockSpec((length, depth), lambda j: (0, 0), pipeline_mode=pl.Buffered(1)),
            pl.BlockSpec((length, tile), lambda j: (0, j)),
        ],
        out_specs=pl.BlockSpec((depth, tile), lambda j: (0, j)),
        scratch_shapes=[pltpu.VMEM((depth, length), BF16)],
        name="weight_grad",
    )(left, right)


def local(
    inputs,
    block_index,
    attention_gain,
    query_norm_gain,
    key_gain,
    feedforward_gain,
    attention_in,
    attention_out,
    gate_up,
    down_weight,
    grad_output,
):
    parts = lax.axis_size("ctx")
    me = lax.axis_index("ctx")
    tokens = inputs.shape[1]
    half_rows = tokens // 2
    length = tokens * parts
    query_heads = QUERY_HEADS // parts
    key_heads = max(1, KEY_VALUE_HEADS // parts)
    copies = key_heads * parts // KEY_VALUE_HEADS
    query_width = query_heads * HEAD_SIZE
    key_width = key_heads * HEAD_SIZE
    all_query = QUERY_HEADS * HEAD_SIZE
    all_key = KEY_VALUE_HEADS * HEAD_SIZE
    hidden_width = FF // parts

    in_width = query_width + 2 * key_width
    own_key = (me // copies) * key_width
    picked_attention = pick_columns(
        [attention_in, attention_out],
        [
            (0, me * query_width, query_width),
            (0, all_query + own_key, key_width),
            (0, all_query + all_key + own_key, key_width),
        ]
        + [(1, (me ^ j) * query_width, query_width) for j in range(parts)],
    )
    weight_attention = gather_plane(picked_attention)
    weight_in = weight_attention[:, :in_width]
    weight_out = weight_attention[:, in_width:]
    own_inputs = inputs[0]
    sequence_inputs = gather_ctx(own_inputs)
    blocks = gather_ctx(block_index[0]).reshape(-1)
    picked_ff = pick_columns(
        [gate_up, down_weight],
        [
            (0, me * hidden_width, hidden_width),
            (0, FF + me * hidden_width, hidden_width),
            (1, me * hidden_width, hidden_width),
        ],
    )
    weight_ff = gather_plane(picked_ff)
    own_grad = grad_output[0]
    later_grad, _ = lax.optimization_barrier((own_grad, sequence_inputs))
    sequence_grad = gather_ctx(later_grad)

    steps_along = jnp.arange(half_rows, dtype=jnp.int32)
    positions = (blocks[:, None] * half_rows + steps_along[None, :]).reshape(-1)
    cosine_table, sine_table = rope_tables(positions)

    rows = sequence_inputs.astype(F32)
    first_scale = rms_scale(rows)
    first_hat = rows * first_scale
    first_normed = (first_hat * attention_gain).astype(BF16)
    projected = rows_by(first_normed, weight_in)
    heads = (query_heads, key_heads)
    shared = [
        projected,
        cosine_table,
        sine_table,
        positions[:, None],
        positions[None, :],
        query_norm_gain[None],
        key_gain[None],
    ]
    attended, logs = attention_call(
        forward_kernel,
        heads,
        shared,
        [
            jax.ShapeDtypeStruct((length, query_width), BF16),
            jax.ShapeDtypeStruct((length, query_heads), F32),
        ],
    )

    all_attended = gather_heads(attended)
    middle = rows + rows_by_t(all_attended, weight_out)
    second_scale = rms_scale(middle)
    second_hat = middle * second_scale
    second_normed = (second_hat * feedforward_gain).astype(BF16)
    own_middle, own_second_hat = middle[:tokens], second_hat[:tokens]
    own_second_scale = second_scale[:tokens]

    weight_gate_up = weight_ff[:, : 2 * hidden_width]
    weight_down = weight_ff[:, 2 * hidden_width :]
    grad_hidden = rows_by(sequence_grad, weight_down)
    gate_values = rows_by(second_normed, weight_gate_up)
    gate = gate_values[:, :hidden_width]
    upward = gate_values[:, hidden_width:]
    sigmoid_gate = jax.nn.sigmoid(gate)
    silu_gate = gate * sigmoid_gate
    hidden = (silu_gate * upward).astype(BF16)
    grad_gate = grad_hidden * upward * sigmoid_gate * (1.0 + gate * (1.0 - sigmoid_gate))
    grad_upward = grad_hidden * silu_gate
    grad_gate_up = jnp.concatenate([grad_gate, grad_upward], axis=1).astype(BF16)
    partial_second = rows_by_t(grad_gate_up, weight_gate_up)
    grad_second = scatter_ctx(partial_second)
    gate_up_weight_grad = weight_grad(second_normed, grad_gate_up)
    down_weight_grad = weight_grad(sequence_grad, hidden)
    gate_up_pieces = scatter_weight(gate_up_weight_grad, scatter_plane)
    down_pieces = scatter_weight(down_weight_grad, scatter_plane_swaps)
    partial_output = rows_by_t(hidden, weight_down)

    feedforward_part = jnp.sum(grad_second * own_second_hat, axis=0)
    grad_middle = own_grad.astype(F32) + rms_back(
        grad_second, own_second_hat, own_second_scale, feedforward_gain
    )
    grad_middle_short = grad_middle.astype(BF16)
    own_attended_grad = rows_by(grad_middle_short, weight_out).astype(BF16)
    attended_grad = tokens_to_heads(own_attended_grad)
    middle_grad_rows = tokens_to_rows(grad_middle_short)
    out_weight_grad = weight_grad(middle_grad_rows, all_attended)
    out_weight_sum = scatter_plane_swaps(out_weight_grad)
    output_sum = scatter_ctx(partial_output)
    output = (own_middle + output_sum).astype(BF16)[None]
    grad_projected, gain_parts = attention_call(
        backward_kernel,
        heads,
        shared + [logs, attended, attended_grad],
        [
            jax.ShapeDtypeStruct((length, in_width), BF16),
            jax.ShapeDtypeStruct((2, HEAD_SIZE), F32),
        ],
    )
    partial_first = rows_by_t(grad_projected, weight_in)
    attention_part = jnp.sum(partial_first * first_hat, axis=0)
    grad_first = scatter_ctx(partial_first)
    in_weight_grad = weight_grad(first_normed, grad_projected)
    in_pieces = scatter_weight(in_weight_grad, scatter_plane_swaps)
    cores = lax.axis_size("fsdp")
    source = (me * cores + lax.axis_index("fsdp")) % parts
    (attention_in_grad,) = join_pieces(
        source,
        in_pieces,
        [
            [
                (0, query_width, 0, 1),
                (query_width, key_width, all_query, copies),
                (query_width + key_width, key_width, all_query + all_key, copies),
            ]
        ],
    )
    out_pieces = [
        out_weight_sum[:, j * query_width : (j + 1) * query_width] for j in range(parts)
    ]
    (attention_out_grad,) = join_pieces(me, out_pieces, [[(0, query_width, 0, 1)]])
    (gate_up_grad,) = join_pieces(
        source, gate_up_pieces, [[(0, hidden_width, 0, 1), (hidden_width, hidden_width, FF, 1)]]
    )
    (down_grad,) = join_pieces(source, down_pieces, [[(0, hidden_width, 0, 1)]])
    input_grad = grad_middle + rms_back(
        grad_first, first_hat[:tokens], first_scale[:tokens], attention_gain
    )
    input_grad = input_grad.astype(BF16)[None]
    gains = sum_everywhere(
        jnp.concatenate([attention_part, gain_parts.reshape(-1), feedforward_part]),
    )
    marks = [D, D + HEAD_SIZE, D + 2 * HEAD_SIZE]
    gain_sums = jnp.split(gains, marks)

    return (
        output,
        input_grad,
        gain_sums[0],
        gain_sums[1],
        gain_sums[2],
        gain_sums[3],
        attention_in_grad,
        attention_out_grad,
        gate_up_grad,
        down_grad,
    )


def solution(mesh):
    tokens = P(("seq", "fsdp"), "ctx", None)
    weight = P(("seq", "fsdp"), None)
    grad = P(("seq", "ctx", "fsdp"), None)
    in_specs = (tokens, tokens, P(), P(), P(), P(), weight, weight, weight, weight, tokens)
    out_specs = (tokens, tokens, P(), P(), P(), P(), grad, grad, grad, grad)
    return jax.shard_map(local, mesh=mesh, in_specs=in_specs, out_specs=out_specs, check_vma=False)
```

```python
import jax
import jax.numpy as jnp
from jax import lax
from jax.experimental import pallas as pl
from jax.experimental.pallas import tpu as pltpu
from jax.sharding import PartitionSpec as P


D = 2048
QUERY_HEADS = 16
KEY_VALUE_HEADS = 8
HEAD_SIZE = 128
FF = 6144

EPS = 1e-06
ROPE_BASE = 1000000.0
MASK_FLOOR = -1e30
F32 = jnp.float32
BF16 = jnp.bfloat16


def rms_scale(values):
    return lax.rsqrt(jnp.mean(values * values, axis=-1, keepdims=True) + EPS)


def rms_back(grad_normed, normed_hat, scale, gain):
    grad_hat = grad_normed * gain
    inner = jnp.mean(grad_hat * normed_hat, axis=-1, keepdims=True)
    return scale * (grad_hat - normed_hat * inner)


def rope_tables(token_positions):
    half = HEAD_SIZE // 2
    rates = jnp.power(F32(ROPE_BASE), jnp.arange(half, dtype=F32) * (-2.0 / HEAD_SIZE))
    angles = token_positions.astype(F32)[:, None] * rates[None, :]
    cosine, sine = jnp.cos(angles), jnp.sin(angles)
    return (
        jnp.concatenate([cosine, cosine], axis=1),
        jnp.concatenate([-sine, sine], axis=1),
    )


def turn(values):
    return pltpu.roll(values, HEAD_SIZE // 2, 1)


def rows_by(left, right):
    return jnp.dot(left, right, preferred_element_type=F32)


def rows_by_t(left, right):
    return lax.dot_general(left, right, (((1,), (1,)), ((), ())), preferred_element_type=F32)


def t_by_rows(left, right):
    return lax.dot_general(left, right, (((0,), (0,)), ((), ())), preferred_element_type=F32)


def swap(values, axis, step):
    return lax.ppermute(values, axis, [(i, i ^ step) for i in range(lax.axis_size(axis))])


def slots(parts):
    order = [0]
    while len(order) < parts:
        order = [2 * k for k in order] + [2 * k + 1 for k in order]
    return order


def gather_ctx(rows):
    blocks = [rows if k == 0 else swap(rows, "ctx", k) for k in slots(lax.axis_size("ctx"))]
    return jnp.concatenate(blocks, axis=0)


def to_relative(rows):
    seqs, cores = lax.axis_size("seq"), lax.axis_size("fsdp")
    core = lax.axis_index("fsdp")
    blocks = rows.reshape(rows.shape[0], seqs, cores, -1)
    parts = [lax.dynamic_slice_in_dim(blocks, core ^ j, 1, axis=2)[:, :, 0] for j in range(cores)]
    return jnp.concatenate(parts, axis=1).reshape(rows.shape)


def from_relative(rows):
    seqs, cores = lax.axis_size("seq"), lax.axis_size("fsdp")
    core = lax.axis_index("fsdp")
    blocks = rows.reshape(rows.shape[0], cores, seqs, -1)
    parts = [lax.dynamic_slice_in_dim(blocks, core ^ j, 1, axis=1)[:, 0] for j in range(cores)]
    return jnp.stack(parts, axis=2).reshape(rows.shape)


def pick_kernel(picks, starts, *refs):
    sources, upper, lower, sems = refs[:-3], refs[-3], refs[-2], refs[-1]
    half = upper.shape[0]
    copies, at = [], 0
    for n, (source, width) in enumerate(picks):
        start = pl.multiple_of(starts[n], HEAD_SIZE)
        for m, out in enumerate((upper, lower)):
            copies.append(
                pltpu.make_async_copy(
                    sources[source].at[pl.ds(m * half, half), pl.ds(start, width)],
                    out.at[:, pl.ds(at, width)],
                    sems.at[2 * n + m],
                )
            )
        at += width
    for copy in copies:
        copy.start()
    for copy in copies:
        copy.wait()


def pick_columns(sources, picks):
    half = sources[0].shape[0] // 2
    starts = jnp.stack([jnp.asarray(start, jnp.int32) for _, start, _ in picks])
    anywhere = pl.BlockSpec(memory_space=pl.ANY)
    shape = jax.ShapeDtypeStruct((half, sum(width for _, _, width in picks)), BF16)
    return pl.pallas_call(
        lambda *refs: pick_kernel([(source, width) for source, _, width in picks], *refs),
        out_shape=[shape, shape],
        in_specs=[pl.BlockSpec(memory_space=pltpu.SMEM)] + [anywhere] * len(sources),
        out_specs=[pl.BlockSpec(memory_space=pltpu.VMEM)] * 2,
        scratch_shapes=[pltpu.SemaphoreType.DMA((2 * len(picks),))],
        name="pick_columns",
    )(starts, *sources)


def assemble_kernel(widths, seq, *refs):
    count = (len(refs) - 3 - len(widths)) // 2
    uppers, lowers = refs[:count], refs[count : 2 * count]
    outs, (held, in_sems, out_sems) = refs[2 * count : -3], refs[-3:]
    half = uppers[0].shape[0]
    loads = []
    for k in range(count):
        for m, pieces in enumerate((uppers, lowers)):
            load = pltpu.make_async_copy(
                pieces[k], held.at[k, pl.ds(m * half, half)], in_sems.at[2 * k + m]
            )
            load.start()
            loads.append(load)
    stores = []
    for k in range(count):
        loads[2 * k].wait()
        loads[2 * k + 1].wait()
        at = pl.multiple_of((seq[0] ^ k) * 2 * half, 2 * half)
        column = 0
        for n, (out, width) in enumerate(zip(outs, widths)):
            store = pltpu.make_async_copy(
                held.at[k, :, pl.ds(column, width)],
                out.at[pl.ds(at, 2 * half)],
                out_sems.at[len(widths) * k + n],
            )
            store.start()
            stores.append(store)
            column += width
    for store in stores:
        store.wait()


def assemble(uppers, lowers, widths):
    count = len(uppers)
    half, width = uppers[0].shape
    anywhere = pl.BlockSpec(memory_space=pl.ANY)
    return pl.pallas_call(
        lambda *refs: assemble_kernel(widths, *refs),
        out_shape=[jax.ShapeDtypeStruct((2 * half * count, w), BF16) for w in widths],
        in_specs=[pl.BlockSpec(memory_space=pltpu.SMEM)] + [anywhere] * (2 * count),
        out_specs=[anywhere] * len(widths),
        scratch_shapes=[
            pltpu.VMEM((count, 2 * half, width), BF16),
            pltpu.SemaphoreType.DMA((2 * count,)),
            pltpu.SemaphoreType.DMA((len(widths) * count,)),
        ],
        name="asm",
    )(lax.axis_index("seq").astype(jnp.int32)[None], *uppers, *lowers)


def gather_plane(upper, lower, widths):
    seqs, cores = lax.axis_size("seq"), lax.axis_size("fsdp")
    bits = [1 << n for n in range(seqs.bit_length() - 1)]
    gathered = []
    for piece, order in ((upper, bits), (lower, bits[::-1])):
        have = {0: piece}
        for bit in order:
            have.update({k ^ bit: swap(have[k], "seq", bit) for k in list(have)})
        gathered.append([have[k] for k in range(seqs)])
    wholes = assemble(*gathered, widths)
    return [
        [whole] + [swap(whole, "fsdp", j) for j in range(1, cores)] for whole in wholes
    ]


def times(rows, weights):
    depth = weights[0].shape[0]
    return sum(
        rows_by(rows[:, j * depth : (j + 1) * depth], weight) for j, weight in enumerate(weights)
    )


def times_t(rows, weights):
    return [rows_by_t(rows, weight) for weight in weights]


def scatter_ctx(partials):
    step = 1
    while step < lax.axis_size("ctx"):
        half = partials[0].shape[0] // 2
        sent = jnp.concatenate([part[half:].astype(BF16) for part in partials], axis=1)
        other = swap(sent, "ctx", step)
        partials = [jnp.concatenate([part[:half] for part in partials], axis=1) + other.astype(F32)]
        step *= 2
    return partials[0]


def scatter_ctx_direct(partials):
    parts = lax.axis_size("ctx")
    tokens = partials.shape[0] // parts
    pieces = []
    for at, slot in enumerate(slots(parts)[1:], 1):
        piece = partials[at * tokens : (at + 1) * tokens].astype(BF16)
        pieces.append(swap(piece, "ctx", slot))
    total = partials[:tokens]
    for piece in pieces:
        total = total + piece.astype(F32)
    return total


def gather_heads(attended):
    parts = lax.axis_size("ctx")
    tokens = attended.shape[0] // parts
    pieces = [attended] + [swap(attended, "ctx", j) for j in range(1, parts)]
    whole = pl.BlockSpec(memory_space=pltpu.VMEM)
    return pl.pallas_call(
        lambda *refs: join_heads_kernel(tokens, *refs),
        out_shape=jax.ShapeDtypeStruct((parts * tokens, parts * attended.shape[1]), BF16),
        in_specs=[whole] * parts,
        out_specs=whole,
        name="jh",
    )(*pieces)


def join_heads_kernel(tokens, *refs):
    pieces, out = refs[:-1], refs[-1]
    width = pieces[0].shape[1]
    order = slots(len(pieces))
    for j, piece in enumerate(pieces):
        for at, slot in enumerate(order):
            there = order.index(slot ^ j) * tokens
            out[at * tokens : (at + 1) * tokens, j * width : (j + 1) * width] = piece[
                there : there + tokens, :
            ]


def tokens_to_heads(rows):
    parts = lax.axis_size("ctx")
    width = rows.shape[1] // parts
    pieces = []
    for k in slots(parts):
        piece = rows[:, k * width : (k + 1) * width]
        pieces.append(piece if k == 0 else swap(piece, "ctx", k))
    return jnp.concatenate(pieces, axis=0)


def tokens_to_rows(rows):
    seqs, ctxs, cores = lax.axis_size("seq"), lax.axis_size("ctx"), lax.axis_size("fsdp")
    me, core = lax.axis_index("ctx"), lax.axis_index("fsdp")
    depth = rows.shape[1]
    width, block = depth // (seqs * ctxs), depth // (seqs * cores)
    pieces = []
    for k in slots(ctxs):
        first = (me ^ k) * width
        start = ((first // block) ^ core) * (depth // cores) + first % block
        blocks = [
            lax.dynamic_slice_in_dim(rows, start + s * block, width, axis=1) for s in range(seqs)
        ]
        piece = jnp.concatenate(blocks, axis=1)
        pieces.append(piece if k == 0 else swap(piece, "ctx", k))
    return jnp.concatenate(pieces, axis=0)


def scatter_plane_swaps(grad):
    seqs, cores = lax.axis_size("seq"), lax.axis_size("fsdp")
    seq, core = lax.axis_index("seq"), lax.axis_index("fsdp")
    rows = grad.shape[0] // (seqs * cores)
    grad = grad.reshape(seqs, cores, rows, grad.shape[1])

    def of_core(k):
        return lax.dynamic_slice_in_dim(grad, core ^ k, 1, axis=1)[:, 0]

    others = []
    for k in range(1, cores):
        others.append(swap(of_core(k), "fsdp", k))
    total = of_core(0).astype(F32)
    for other in others:
        total = total + other.astype(F32)
    short = total.astype(BF16)
    others = []
    for k in range(1, seqs):
        piece = lax.dynamic_slice_in_dim(short, seq ^ k, 1, axis=0)[0]
        others.append(swap(piece, "seq", k))
    out = lax.dynamic_slice_in_dim(total, seq, 1, axis=0)[0]
    for other in others:
        out = out + other.astype(F32)
    return out.astype(BF16)


def scatter_halves(halves):
    seqs = lax.axis_size("seq")
    seq = lax.axis_index("seq")
    others = [swap(half, "fsdp", j) for j, half in enumerate(halves[1:], 1)]
    total = halves[0].astype(F32)
    for other in others:
        total = total + other.astype(F32)
    total = total.astype(BF16)
    rows = total.shape[0] // seqs
    bits = [1 << n for n in range(seqs.bit_length() - 1)]
    states = []
    for m in range(2):
        at = [(seq ^ k) * rows + m * (rows // 2) for k in range(seqs)]
        states.append(
            {k: lax.dynamic_slice_in_dim(total, at[k], rows // 2, axis=0) for k in range(seqs)}
        )
    for phase in range(len(bits)):
        for m, order in enumerate((bits, bits[::-1])):
            state, bit = states[m], order[phase]
            sent = [k for k in sorted(state) if k & bit]
            piece = jnp.concatenate([state[k].astype(BF16) for k in sent], axis=0)
            piece = swap(piece, "seq", bit)
            last = phase + 1 == len(bits)
            states[m] = {
                k ^ bit: state[k ^ bit].astype(F32)
                + piece[n * (rows // 2) : (n + 1) * (rows // 2)].astype(F32)
                for n, k in enumerate(sent)
            }
            if not last:
                states[m] = lax.optimization_barrier(states[m])
    return jnp.concatenate([state[0].astype(BF16) for state in states], axis=0)


def scatter_plane(grad):
    return lax.psum_scatter(grad, ("fsdp", "seq"), scatter_dimension=0, tiled=True)


def exchange(grad):
    ctxs, cores = lax.axis_size("ctx"), lax.axis_size("fsdp")
    ctx = lax.axis_index("ctx")
    rows = grad.shape[0] // ctxs
    pieces = []
    for k in range(ctxs):
        piece = lax.dynamic_slice_in_dim(grad, (ctx ^ k) * rows, rows, axis=0)
        pairs = [
            (c * cores + f, f * ctxs + (c ^ k)) for c in range(ctxs) for f in range(cores)
        ]
        pieces.append(lax.ppermute(piece, ("ctx", "fsdp"), pairs))
    return pieces


def scatter_weight(grad, over_plane):
    return exchange(over_plane(grad))


def sum_everywhere(values):
    for axis in ("ctx", "seq", "fsdp"):
        size = lax.axis_size(axis)
        sums = [values] + [swap(values, axis, k) for k in range(1, size)]
        while len(sums) > 1:
            sums = [sums[i] + sums[i + 1] for i in range(0, len(sums), 2)]
        values = sums[0]
    return values


def join_kernel(segments, source_ref, *refs):
    pieces, outs = refs[: -len(segments)], refs[-len(segments) :]
    for out, group in zip(outs, segments):
        if any(copies > 1 for _, _, _, copies in group):
            out[...] = jnp.zeros_like(out)
    for k, piece in enumerate(pieces):
        owner = source_ref[0] ^ k
        for out, group in zip(outs, segments):
            for start, width, base, copies in group:
                at = pl.multiple_of(base + (owner // copies) * width, HEAD_SIZE)
                values = piece[:, start : start + width].astype(F32)
                if copies > 1:
                    values = values + out[:, pl.ds(at, width)]
                out[:, pl.ds(at, width)] = values


def join_pieces(source, pieces, segments):
    rows = pieces[0].shape[0]
    widths = [
        sum(width * len(pieces) // copies for _, width, _, copies in group) for group in segments
    ]
    whole = pl.BlockSpec(memory_space=pltpu.VMEM)
    return pl.pallas_call(
        lambda *refs: join_kernel(segments, *refs),
        out_shape=[jax.ShapeDtypeStruct((rows, width), F32) for width in widths],
        in_specs=[pl.BlockSpec(memory_space=pltpu.SMEM)] + [whole] * len(pieces),
        out_specs=[whole] * len(segments),
        name="join_pieces",
    )(source.astype(jnp.int32)[None], *pieces)


def head_columns(ref, head):
    return ref[:, head * HEAD_SIZE : (head + 1) * HEAD_SIZE]


def normalized(values):
    scale = lax.rsqrt(jnp.mean(values * values, axis=-1, keepdims=True) + EPS)
    return values * scale, scale


def rotated(normed, cosine, sine):
    return (normed * cosine + turn(normed) * sine).astype(BF16)


def row_blocks(length):
    step = min(length, 512)
    return [(at, step) for at in range(0, length, step)]


def forward_kernel(query_heads, key_heads, *refs):
    (projected, cosine_ref, sine_ref, column, row, query_gain, key_gain, attended, logs) = refs
    cosine, sine = cosine_ref[...], sine_ref[...]
    group = query_heads // key_heads
    scale = HEAD_SIZE ** (-0.5)
    length = projected.shape[0]
    for key_head in range(key_heads):
        key_hat, _ = normalized(head_columns(projected, query_heads + key_head))
        key = rotated(key_hat * key_gain[...], cosine, sine)
        value = head_columns(projected, query_heads + key_heads + key_head).astype(BF16)
        for head in range(key_head * group, (key_head + 1) * group):
            query_hat, _ = normalized(head_columns(projected, head))
            query = rotated(query_hat * query_gain[...], cosine, sine)
            for at, step in row_blocks(length):
                scores = rows_by_t(query[at : at + step], key) * scale
                allowed = row[...] <= column[at : at + step, :]
                scores = jnp.where(allowed, scores, MASK_FLOOR)
                peak = jnp.max(scores, axis=-1, keepdims=True)
                total = jnp.sum(jnp.exp(scores - peak), axis=-1, keepdims=True)
                log_total = peak + jnp.log(total)
                weights = jnp.exp(scores - log_total).astype(BF16)
                attended[at : at + step, head * HEAD_SIZE : (head + 1) * HEAD_SIZE] = rows_by(
                    weights, value
                ).astype(BF16)
                logs[at : at + step, head : head + 1] = log_total


def backward_kernel(query_heads, key_heads, *refs):
    (
        projected,
        cosine_ref,
        sine_ref,
        column,
        row,
        query_gain,
        key_gain,
        logs,
        attended,
        attended_grad,
        grad_projected,
        gain_parts,
    ) = refs
    cosine, sine = cosine_ref[...], sine_ref[...]
    group = query_heads // key_heads
    scale = HEAD_SIZE ** (-0.5)
    length = projected.shape[0]
    query_part = jnp.zeros((1, HEAD_SIZE), F32)
    key_part = jnp.zeros((1, HEAD_SIZE), F32)

    def finish(grad_rotary, hat, factor, gain):
        grad = grad_rotary * scale
        unrotated = grad * cosine - turn(grad) * sine
        part = jnp.sum(unrotated * hat, axis=0, keepdims=True)
        grad_hat = unrotated * gain
        inner = jnp.mean(grad_hat * hat, axis=-1, keepdims=True)
        return (factor * (grad_hat - hat * inner)).astype(BF16), part

    def store(head, values):
        grad_projected[:, head * HEAD_SIZE : (head + 1) * HEAD_SIZE] = values

    for key_head in range(key_heads):
        key_hat, key_scale = normalized(head_columns(projected, query_heads + key_head))
        key = rotated(key_hat * key_gain[...], cosine, sine)
        value = head_columns(projected, query_heads + key_heads + key_head).astype(BF16)
        key_acc = jnp.zeros((length, HEAD_SIZE), F32)
        value_acc = jnp.zeros((length, HEAD_SIZE), F32)
        for head in range(key_head * group, (key_head + 1) * group):
            query_hat, query_scale = normalized(head_columns(projected, head))
            query = rotated(query_hat * query_gain[...], cosine, sine)
            grad = head_columns(attended_grad, head)
            delta = jnp.sum(
                grad.astype(F32) * head_columns(attended, head).astype(F32), axis=-1, keepdims=True
            )
            query_accs = []
            for at, step in row_blocks(length):
                rows = slice(at, at + step)
                scores = rows_by_t(query[rows], key) * scale
                allowed = row[...] <= column[rows, :]
                scores = jnp.where(allowed, scores, MASK_FLOOR)
                probs = jnp.exp(scores - logs[rows, head : head + 1])
                grad_probs = rows_by_t(grad[rows], value)
                grad_scores = (probs * (grad_probs - delta[rows])).astype(BF16)
                query_accs.append(rows_by(grad_scores, key))
                key_acc = key_acc + t_by_rows(grad_scores, query[rows])
                value_acc = value_acc + t_by_rows(probs.astype(BF16), grad[rows])
            query_acc = jnp.concatenate(query_accs, axis=0)
            grads, part = finish(query_acc, query_hat, query_scale, query_gain[...])
            query_part = query_part + part
            store(head, grads)
        grads, part = finish(key_acc, key_hat, key_scale, key_gain[...])
        key_part = key_part + part
        store(query_heads + key_head, grads)
        store(query_heads + key_heads + key_head, value_acc.astype(BF16))
    gain_parts[0:1, :] = query_part
    gain_parts[1:2, :] = key_part


def attention_call(kernel, heads, operands, outs):
    whole = pl.BlockSpec(memory_space=pltpu.VMEM)
    return pl.pallas_call(
        lambda *refs: kernel(*heads, *refs),
        out_shape=outs,
        in_specs=[whole] * len(operands),
        out_specs=[whole] * len(outs),
    )(*operands)


def weight_grad_kernel(left, right, *refs):
    outs, turned = refs[:-1], refs[-1]

    @pl.when(pl.program_id(0) == 0)
    def _():
        turned[...] = left[...].T

    rows = outs[0].shape[0]
    for j, out in enumerate(outs):
        out[...] = rows_by(turned[j * rows : (j + 1) * rows], right[...]).astype(BF16)


def weight_grad(left, right, count=1):
    length, depth = left.shape
    width = right.shape[1]
    tile = HEAD_SIZE * 4 if width % (HEAD_SIZE * 4) == 0 else HEAD_SIZE
    return pl.pallas_call(
        weight_grad_kernel,
        grid=(width // tile,),
        out_shape=[jax.ShapeDtypeStruct((depth // count, width), BF16)] * count,
        in_specs=[
            pl.BlockSpec((length, depth), lambda j: (0, 0), pipeline_mode=pl.Buffered(1)),
            pl.BlockSpec((length, tile), lambda j: (0, j)),
        ],
        out_specs=[pl.BlockSpec((depth // count, tile), lambda j: (0, j))] * count,
        scratch_shapes=[pltpu.VMEM((depth, length), BF16)],
        name="weight_grad",
    )(left, right)


def weight_grad_sorted_kernel(cores, core, left, right, out, turned):
    rows = turned.shape[0] // cores

    @pl.when(pl.program_id(0) == 0)
    def _():
        for j in range(cores):
            at = pl.multiple_of((core[0] ^ j) * rows, rows)
            turned[pl.ds(at, rows)] = left[:, j * rows : (j + 1) * rows].T

    out[...] = rows_by(turned[...], right[...]).astype(BF16)


def weight_grad_sorted(left, right):
    cores = lax.axis_size("fsdp")
    length, depth = left.shape
    width = right.shape[1]
    tile = HEAD_SIZE * 4 if width % (HEAD_SIZE * 4) == 0 else HEAD_SIZE
    return pl.pallas_call(
        lambda *refs: weight_grad_sorted_kernel(cores, *refs),
        grid=(width // tile,),
        out_shape=jax.ShapeDtypeStruct((depth, width), BF16),
        in_specs=[
            pl.BlockSpec(memory_space=pltpu.SMEM),
            pl.BlockSpec((length, depth), lambda t: (0, 0), pipeline_mode=pl.Buffered(1)),
            pl.BlockSpec((length, tile), lambda t: (0, t)),
        ],
        out_specs=pl.BlockSpec((depth, tile), lambda t: (0, t)),
        scratch_shapes=[pltpu.VMEM((depth, length), BF16)],
        name="weight_grad",
    )(lax.axis_index("fsdp").astype(jnp.int32)[None], left, right)


def local(
    inputs,
    block_index,
    attention_gain,
    query_norm_gain,
    key_gain,
    feedforward_gain,
    attention_in,
    attention_out,
    gate_up,
    down_weight,
    grad_output,
):
    parts, cores = lax.axis_size("ctx"), lax.axis_size("fsdp")
    me = lax.axis_index("ctx")
    tokens = inputs.shape[1]
    half_rows = tokens // 2
    length = tokens * parts
    query_heads = QUERY_HEADS // parts
    key_heads = max(1, KEY_VALUE_HEADS // parts)
    copies = key_heads * parts // KEY_VALUE_HEADS
    query_width = query_heads * HEAD_SIZE
    key_width = key_heads * HEAD_SIZE
    all_query = QUERY_HEADS * HEAD_SIZE
    all_key = KEY_VALUE_HEADS * HEAD_SIZE
    hidden_width = FF // parts

    in_width = query_width + 2 * key_width
    own_key = (me // copies) * key_width
    own_inputs = to_relative(inputs[0])
    sequence_inputs = gather_ctx(own_inputs)
    blocks = gather_ctx(block_index[0]).reshape(-1)
    own_grad = to_relative(grad_output[0])
    sequence_grad = gather_ctx(own_grad)
    first_gain, second_gain = (
        to_relative(gain[None])[0] for gain in (attention_gain, feedforward_gain)
    )

    picked_in = pick_columns(
        [attention_in],
        [
            (0, me * query_width, query_width),
            (0, all_query + own_key, key_width),
            (0, all_query + all_key + own_key, key_width),
        ],
    )
    (weight_in,) = gather_plane(*picked_in, [in_width])
    picked_out = pick_columns(
        [attention_out], [(0, (me ^ j) * query_width, query_width) for j in range(parts)]
    )
    (weight_out,) = gather_plane(*picked_out, [all_query])
    picked_ff = pick_columns(
        [gate_up, down_weight],
        [
            (0, me * hidden_width, hidden_width),
            (0, FF + me * hidden_width, hidden_width),
            (1, me * hidden_width, hidden_width),
        ],
    )
    weight_gate_up, weight_down = gather_plane(*picked_ff, [2 * hidden_width, hidden_width])

    steps_along = jnp.arange(half_rows, dtype=jnp.int32)
    positions = (blocks[:, None] * half_rows + steps_along[None, :]).reshape(-1)
    cosine_table, sine_table = rope_tables(positions)

    rows = sequence_inputs.astype(F32)
    first_scale = rms_scale(rows)
    first_hat = rows * first_scale
    first_normed = (first_hat * first_gain).astype(BF16)
    projected = times(first_normed, weight_in)
    heads = (query_heads, key_heads)
    shared = [
        projected,
        cosine_table,
        sine_table,
        positions[:, None],
        positions[None, :],
        query_norm_gain[None],
        key_gain[None],
    ]
    attended, logs = attention_call(
        forward_kernel,
        heads,
        shared,
        [
            jax.ShapeDtypeStruct((length, query_width), BF16),
            jax.ShapeDtypeStruct((length, query_heads), F32),
        ],
    )

    all_attended = gather_heads(attended)
    middle = rows + jnp.concatenate(times_t(all_attended, weight_out), axis=1)
    second_scale = rms_scale(middle)
    second_hat = middle * second_scale
    second_normed = (second_hat * second_gain).astype(BF16)
    own_middle, own_second_hat = middle[:tokens], second_hat[:tokens]
    own_second_scale = second_scale[:tokens]

    grad_hidden = times(sequence_grad, weight_down)
    gate_values = times(second_normed, weight_gate_up)
    gate = gate_values[:, :hidden_width]
    upward = gate_values[:, hidden_width:]
    sigmoid_gate = jax.nn.sigmoid(gate)
    silu_gate = gate * sigmoid_gate
    hidden = (silu_gate * upward).astype(BF16)
    grad_gate = grad_hidden * upward * sigmoid_gate * (1.0 + gate * (1.0 - sigmoid_gate))
    grad_upward = grad_hidden * silu_gate
    grad_gate_up = jnp.concatenate([grad_gate, grad_upward], axis=1).astype(BF16)
    grad_second = jnp.concatenate(
        [
            scatter_ctx_direct(lax.optimization_barrier(rows_by_t(grad_gate_up, weight)))
            for weight in weight_gate_up
        ],
        axis=1,
    )
    gate_up_weight_grad = weight_grad_sorted(second_normed, grad_gate_up)
    down_weight_grad = weight_grad(sequence_grad, hidden, cores)
    gate_up_pieces = scatter_weight(gate_up_weight_grad, scatter_plane)
    down_pieces = scatter_weight(down_weight_grad, scatter_halves)
    partial_output = times_t(hidden, weight_down)

    feedforward_part = jnp.sum(grad_second * own_second_hat, axis=0)
    grad_middle = own_grad.astype(F32) + rms_back(
        grad_second, own_second_hat, own_second_scale, second_gain
    )
    grad_middle_short = grad_middle.astype(BF16)
    own_attended_grad = times(grad_middle_short, weight_out).astype(BF16)
    attended_grad = tokens_to_heads(own_attended_grad)
    middle_grad_rows = tokens_to_rows(grad_middle_short)
    (out_weight_grad,) = weight_grad(middle_grad_rows, all_attended)
    out_weight_sum = scatter_plane_swaps(out_weight_grad)
    output_sum = scatter_ctx(partial_output)
    output = from_relative((own_middle + output_sum).astype(BF16))[None]
    grad_projected, gain_parts = attention_call(
        backward_kernel,
        heads,
        shared + [logs, attended, attended_grad],
        [
            jax.ShapeDtypeStruct((length, in_width), BF16),
            jax.ShapeDtypeStruct((2, HEAD_SIZE), F32),
        ],
    )
    partial_first = times_t(grad_projected, weight_in)
    depth = D // cores
    attention_part = jnp.concatenate(
        [
            jnp.sum(part * first_hat[:, j * depth : (j + 1) * depth], axis=0)
            for j, part in enumerate(partial_first)
        ]
    )
    grad_first = scatter_ctx(partial_first)
    in_weight_grad = weight_grad(first_normed, grad_projected, cores)
    in_pieces = scatter_weight(in_weight_grad, scatter_halves)
    source = (me * cores + lax.axis_index("fsdp")) % parts
    (attention_in_grad,) = join_pieces(
        source,
        in_pieces,
        [
            [
                (0, query_width, 0, 1),
                (query_width, key_width, all_query, copies),
                (query_width + key_width, key_width, all_query + all_key, copies),
            ]
        ],
    )
    out_pieces = [
        out_weight_sum[:, j * query_width : (j + 1) * query_width] for j in range(parts)
    ]
    (attention_out_grad,) = join_pieces(
        me, out_pieces, [[(0, query_width, 0, 1)]])
    (gate_up_grad,) = join_pieces(
        source,
        gate_up_pieces, [[(0, hidden_width, 0, 1), (hidden_width, hidden_width, FF, 1)]]
    )
    (down_grad,) = join_pieces(
        source, down_pieces, [[(0, hidden_width, 0, 1)]])
    input_grad = grad_middle + rms_back(
        grad_first, first_hat[:tokens], first_scale[:tokens], first_gain
    )
    input_grad = from_relative(input_grad.astype(BF16))[None]
    gains = sum_everywhere(
        jnp.concatenate(
            [
                from_relative(attention_part[None])[0],
                gain_parts.reshape(-1),
                from_relative(feedforward_part[None])[0],
            ]
        ),
    )
    marks = [D, D + HEAD_SIZE, D + 2 * HEAD_SIZE]
    gain_sums = jnp.split(gains, marks)

    return (
        output,
        input_grad,
        gain_sums[0],
        gain_sums[1],
        gain_sums[2],
        gain_sums[3],
        attention_in_grad,
        attention_out_grad,
        gate_up_grad,
        down_grad,
    )


def solution(mesh):
    tokens = P(("seq", "fsdp"), "ctx", None)
    weight = P(("seq", "fsdp"), None)
    grad = P(("seq", "ctx", "fsdp"), None)
    in_specs = (tokens, tokens, P(), P(), P(), P(), weight, weight, weight, weight, tokens)
    out_specs = (tokens, tokens, P(), P(), P(), P(), grad, grad, grad, grad)
    return jax.shard_map(local, mesh=mesh, in_specs=in_specs, out_specs=out_specs, check_vma=False)
```

```python
import jax
import jax.numpy as jnp
from jax import lax
from jax.experimental import pallas as pl
from jax.experimental.pallas import tpu as pltpu
from jax.sharding import PartitionSpec as P


D = 2048
QUERY_HEADS = 16
KEY_VALUE_HEADS = 8
HEAD_SIZE = 128
FF = 6144

EPS = 1e-06
ROPE_BASE = 1000000.0
MASK_FLOOR = -1e30
F32 = jnp.float32
BF16 = jnp.bfloat16


def rms_scale(values):
    return lax.rsqrt(jnp.mean(values * values, axis=-1, keepdims=True) + EPS)


def rms_back(grad_normed, normed_hat, scale, gain):
    grad_hat = grad_normed * gain
    inner = jnp.mean(grad_hat * normed_hat, axis=-1, keepdims=True)
    return scale * (grad_hat - normed_hat * inner)


def rope_tables(token_positions):
    half = HEAD_SIZE // 2
    rates = jnp.power(F32(ROPE_BASE), jnp.arange(half, dtype=F32) * (-2.0 / HEAD_SIZE))
    angles = token_positions.astype(F32)[:, None] * rates[None, :]
    cosine, sine = jnp.cos(angles), jnp.sin(angles)
    return (
        jnp.concatenate([cosine, cosine], axis=1),
        jnp.concatenate([-sine, sine], axis=1),
    )


def turn(values):
    return pltpu.roll(values, HEAD_SIZE // 2, 1)


def rows_by(left, right):
    return jnp.dot(left, right, preferred_element_type=F32)


def rows_by_t(left, right):
    return lax.dot_general(left, right, (((1,), (1,)), ((), ())), preferred_element_type=F32)


def t_by_rows(left, right):
    return lax.dot_general(left, right, (((0,), (0,)), ((), ())), preferred_element_type=F32)


def swap(values, axis, step):
    return lax.ppermute(values, axis, [(i, i ^ step) for i in range(lax.axis_size(axis))])


def slots(parts):
    order = [0]
    while len(order) < parts:
        order = [2 * k for k in order] + [2 * k + 1 for k in order]
    return order


def gather_ctx(rows):
    blocks = [rows if k == 0 else swap(rows, "ctx", k) for k in slots(lax.axis_size("ctx"))]
    return jnp.concatenate(blocks, axis=0)


def to_relative(rows):
    seqs, cores = lax.axis_size("seq"), lax.axis_size("fsdp")
    core = lax.axis_index("fsdp")
    blocks = rows.reshape(rows.shape[0], seqs, cores, -1)
    parts = [lax.dynamic_slice_in_dim(blocks, core ^ j, 1, axis=2)[:, :, 0] for j in range(cores)]
    return jnp.concatenate(parts, axis=1).reshape(rows.shape)


def from_relative(rows):
    seqs, cores = lax.axis_size("seq"), lax.axis_size("fsdp")
    core = lax.axis_index("fsdp")
    blocks = rows.reshape(rows.shape[0], cores, seqs, -1)
    parts = [lax.dynamic_slice_in_dim(blocks, core ^ j, 1, axis=1)[:, 0] for j in range(cores)]
    return jnp.stack(parts, axis=2).reshape(rows.shape)


def pick_kernel(picks, starts, *refs):
    sources, upper, lower, sems = refs[:-3], refs[-3], refs[-2], refs[-1]
    half = upper.shape[0]
    copies, at = [], 0
    for n, (source, width) in enumerate(picks):
        start = pl.multiple_of(starts[n], HEAD_SIZE)
        for m, out in enumerate((upper, lower)):
            copies.append(
                pltpu.make_async_copy(
                    sources[source].at[pl.ds(m * half, half), pl.ds(start, width)],
                    out.at[:, pl.ds(at, width)],
                    sems.at[2 * n + m],
                )
            )
        at += width
    for copy in copies:
        copy.start()
    for copy in copies:
        copy.wait()


def pick_columns(sources, picks):
    half = sources[0].shape[0] // 2
    starts = jnp.stack([jnp.asarray(start, jnp.int32) for _, start, _ in picks])
    anywhere = pl.BlockSpec(memory_space=pl.ANY)
    shape = jax.ShapeDtypeStruct((half, sum(width for _, _, width in picks)), BF16)
    return pl.pallas_call(
        lambda *refs: pick_kernel([(source, width) for source, _, width in picks], *refs),
        out_shape=[shape, shape],
        in_specs=[pl.BlockSpec(memory_space=pltpu.SMEM)] + [anywhere] * len(sources),
        out_specs=[pl.BlockSpec(memory_space=pltpu.VMEM)] * 2,
        scratch_shapes=[pltpu.SemaphoreType.DMA((2 * len(picks),))],
        name="pick_columns",
    )(starts, *sources)


def assemble_kernel(places, widths, seq, *refs):
    outs, (held, in_sems, out_sems) = refs[-3 - len(widths) : -3], refs[-3:]
    pieces = refs[-3 - len(widths) - len(places) : -3 - len(widths)]
    half = pieces[0].shape[0]
    loads = []
    for n, piece in enumerate(pieces):
        load = pltpu.make_async_copy(piece, held.at[n], in_sems.at[n])
        load.start()
        loads.append(load)
    stores = []
    for n, (slot, m) in enumerate(places):
        loads[n].wait()
        at = pl.multiple_of((seq[0] ^ slot) * 2 * half + m * half, half)
        column = 0
        for w, (out, width) in enumerate(zip(outs, widths)):
            store = pltpu.make_async_copy(
                held.at[n, :, pl.ds(column, width)],
                out.at[pl.ds(at, half)],
                out_sems.at[len(widths) * n + w],
            )
            store.start()
            stores.append(store)
            column += width
    for store in stores:
        store.wait()


def assemble(pieces, rows, widths, base=()):
    places = list(pieces)
    arrays = [pieces[place] for place in places]
    anywhere = pl.BlockSpec(memory_space=pl.ANY)
    return pl.pallas_call(
        lambda *refs: assemble_kernel(places, widths, *refs),
        out_shape=[jax.ShapeDtypeStruct((rows, w), BF16) for w in widths],
        in_specs=[pl.BlockSpec(memory_space=pltpu.SMEM)]
        + [anywhere] * (len(base) + len(arrays)),
        out_specs=[anywhere] * len(widths),
        scratch_shapes=[
            pltpu.VMEM((len(arrays),) + arrays[0].shape, BF16),
            pltpu.SemaphoreType.DMA((len(arrays),)),
            pltpu.SemaphoreType.DMA((len(widths) * len(arrays),)),
        ],
        input_output_aliases={1 + n: n for n in range(len(base))},
        name="asm",
    )(lax.axis_index("seq").astype(jnp.int32)[None], *base, *arrays)


def gather_plane(upper, lower, widths, early=False):
    seqs, cores = lax.axis_size("seq"), lax.axis_size("fsdp")
    bits = [1 << n for n in range(seqs.bit_length() - 1)]
    have = {(0, 0): upper, (0, 1): lower}
    wholes, done = (), set()
    rows = 2 * seqs * upper.shape[0]
    for phase in range(len(bits)):
        if early and phase == len(bits) - 1:
            wholes = assemble(have, rows, widths)
            done = set(have)
        for k, m in list(have):
            bit = bits[phase] if m == 0 else bits[-1 - phase]
            have[k ^ bit, m] = swap(have[k, m], "seq", bit)
    rest = {place: piece for place, piece in have.items() if place not in done}
    wholes = assemble(rest, rows, widths, wholes)
    return [
        [whole] + [swap(whole, "fsdp", j) for j in range(1, cores)] for whole in wholes
    ]


def times(rows, weights, apart=False):
    depth = weights[0].shape[0]
    total = rows_by(rows[:, :depth], weights[0])
    if apart:
        total = lax.optimization_barrier(total)
    for j, weight in enumerate(weights[1:], 1):
        total = total + rows_by(rows[:, j * depth : (j + 1) * depth], weight)
    return total


def times_t(rows, weights):
    return [rows_by_t(rows, weight) for weight in weights]


def scatter_ctx(partials):
    step = 1
    while step < lax.axis_size("ctx"):
        half = partials[0].shape[0] // 2
        sent = jnp.concatenate([part[half:].astype(BF16) for part in partials], axis=1)
        other = swap(sent, "ctx", step)
        partials = [jnp.concatenate([part[:half] for part in partials], axis=1) + other.astype(F32)]
        step *= 2
    return partials[0]


def scatter_ctx_direct(partials):
    parts = lax.axis_size("ctx")
    tokens = partials.shape[0] // parts
    pieces = []
    for at, slot in enumerate(slots(parts)[1:], 1):
        piece = partials[at * tokens : (at + 1) * tokens].astype(BF16)
        pieces.append(swap(piece, "ctx", slot))
    total = partials[:tokens]
    for piece in pieces:
        total = total + piece.astype(F32)
    return total


def gather_heads(attended):
    parts = lax.axis_size("ctx")
    tokens = attended.shape[0] // parts
    pieces = [attended] + [swap(attended, "ctx", j) for j in range(1, parts)]
    whole = pl.BlockSpec(memory_space=pltpu.VMEM)
    return pl.pallas_call(
        lambda *refs: join_heads_kernel(tokens, *refs),
        out_shape=jax.ShapeDtypeStruct((parts * tokens, parts * attended.shape[1]), BF16),
        in_specs=[whole] * parts,
        out_specs=whole,
        name="jh",
    )(*pieces)


def join_heads_kernel(tokens, *refs):
    pieces, out = refs[:-1], refs[-1]
    width = pieces[0].shape[1]
    order = slots(len(pieces))
    for j, piece in enumerate(pieces):
        for at, slot in enumerate(order):
            there = order.index(slot ^ j) * tokens
            out[at * tokens : (at + 1) * tokens, j * width : (j + 1) * width] = piece[
                there : there + tokens, :
            ]


def tokens_to_heads(rows):
    parts = lax.axis_size("ctx")
    width = rows.shape[1] // parts
    pieces = []
    for k in slots(parts):
        piece = rows[:, k * width : (k + 1) * width]
        pieces.append(piece if k == 0 else swap(piece, "ctx", k))
    return jnp.concatenate(pieces, axis=0)


def tokens_to_rows(rows):
    seqs, ctxs, cores = lax.axis_size("seq"), lax.axis_size("ctx"), lax.axis_size("fsdp")
    me, core = lax.axis_index("ctx"), lax.axis_index("fsdp")
    depth = rows.shape[1]
    width, block = depth // (seqs * ctxs), depth // (seqs * cores)
    pieces = []
    for k in slots(ctxs):
        first = (me ^ k) * width
        start = ((first // block) ^ core) * (depth // cores) + first % block
        blocks = [
            lax.dynamic_slice_in_dim(rows, start + s * block, width, axis=1) for s in range(seqs)
        ]
        piece = jnp.concatenate(blocks, axis=1)
        pieces.append(piece if k == 0 else swap(piece, "ctx", k))
    return jnp.concatenate(pieces, axis=0)


def scatter_plane_swaps(grad):
    seqs, cores = lax.axis_size("seq"), lax.axis_size("fsdp")
    seq, core = lax.axis_index("seq"), lax.axis_index("fsdp")
    rows = grad.shape[0] // (seqs * cores)
    grad = grad.reshape(seqs, cores, rows, grad.shape[1])

    def of_core(k):
        return lax.dynamic_slice_in_dim(grad, core ^ k, 1, axis=1)[:, 0]

    others = []
    for k in range(1, cores):
        others.append(swap(of_core(k), "fsdp", k))
    total = of_core(0).astype(F32)
    for other in others:
        total = total + other.astype(F32)
    short = total.astype(BF16)
    others = []
    for k in range(1, seqs):
        piece = lax.dynamic_slice_in_dim(short, seq ^ k, 1, axis=0)[0]
        others.append(swap(piece, "seq", k))
    out = lax.dynamic_slice_in_dim(total, seq, 1, axis=0)[0]
    for other in others:
        out = out + other.astype(F32)
    return out.astype(BF16)


def scatter_halves(halves):
    seqs = lax.axis_size("seq")
    seq = lax.axis_index("seq")
    others = [swap(half, "fsdp", j) for j, half in enumerate(halves[1:], 1)]
    total = halves[0].astype(F32)
    for other in others:
        total = total + other.astype(F32)
    total = total.astype(BF16)
    rows = total.shape[0] // seqs
    bits = [1 << n for n in range(seqs.bit_length() - 1)]
    states = []
    for m in range(2):
        at = [(seq ^ k) * rows + m * (rows // 2) for k in range(seqs)]
        states.append(
            {k: lax.dynamic_slice_in_dim(total, at[k], rows // 2, axis=0) for k in range(seqs)}
        )
    for phase in range(len(bits)):
        for m, order in enumerate((bits, bits[::-1])):
            state, bit = states[m], order[phase]
            sent = [k for k in sorted(state) if k & bit]
            piece = jnp.concatenate([state[k].astype(BF16) for k in sent], axis=0)
            piece = swap(piece, "seq", bit)
            last = phase + 1 == len(bits)
            states[m] = {
                k ^ bit: state[k ^ bit].astype(F32)
                + piece[n * (rows // 2) : (n + 1) * (rows // 2)].astype(F32)
                for n, k in enumerate(sent)
            }
            if not last:
                states[m] = lax.optimization_barrier(states[m])
    return jnp.concatenate([state[0].astype(BF16) for state in states], axis=0)


def scatter_plane(grad):
    return lax.psum_scatter(grad, ("fsdp", "seq"), scatter_dimension=0, tiled=True)


def exchange(grad):
    ctxs, cores = lax.axis_size("ctx"), lax.axis_size("fsdp")
    ctx = lax.axis_index("ctx")
    rows = grad.shape[0] // ctxs
    pieces = []
    for k in range(ctxs):
        piece = lax.dynamic_slice_in_dim(grad, (ctx ^ k) * rows, rows, axis=0)
        pairs = [
            (c * cores + f, f * ctxs + (c ^ k)) for c in range(ctxs) for f in range(cores)
        ]
        pieces.append(lax.ppermute(piece, ("ctx", "fsdp"), pairs))
    return pieces


def scatter_weight(grad, over_plane):
    return exchange(over_plane(grad))


def sum_everywhere(values):
    for axis in ("ctx", "seq", "fsdp"):
        size = lax.axis_size(axis)
        sums = [values] + [swap(values, axis, k) for k in range(1, size)]
        while len(sums) > 1:
            sums = [sums[i] + sums[i + 1] for i in range(0, len(sums), 2)]
        values = sums[0]
    return values


def join_kernel(segments, source_ref, *refs):
    pieces, outs = refs[: -len(segments)], refs[-len(segments) :]
    for out, group in zip(outs, segments):
        if any(copies > 1 for _, _, _, copies in group):
            out[...] = jnp.zeros_like(out)
    for k, piece in enumerate(pieces):
        owner = source_ref[0] ^ k
        for out, group in zip(outs, segments):
            for start, width, base, copies in group:
                at = pl.multiple_of(base + (owner // copies) * width, HEAD_SIZE)
                values = piece[:, start : start + width].astype(F32)
                if copies > 1:
                    values = values + out[:, pl.ds(at, width)]
                out[:, pl.ds(at, width)] = values


def join_pieces(source, pieces, segments):
    rows = pieces[0].shape[0]
    widths = [
        sum(width * len(pieces) // copies for _, width, _, copies in group) for group in segments
    ]
    whole = pl.BlockSpec(memory_space=pltpu.VMEM)
    return pl.pallas_call(
        lambda *refs: join_kernel(segments, *refs),
        out_shape=[jax.ShapeDtypeStruct((rows, width), F32) for width in widths],
        in_specs=[pl.BlockSpec(memory_space=pltpu.SMEM)] + [whole] * len(pieces),
        out_specs=[whole] * len(segments),
        name="join_pieces",
    )(source.astype(jnp.int32)[None], *pieces)


def head_columns(ref, head):
    return ref[:, head * HEAD_SIZE : (head + 1) * HEAD_SIZE]


def normalized(values):
    scale = lax.rsqrt(jnp.mean(values * values, axis=-1, keepdims=True) + EPS)
    return values * scale, scale


def rotated(normed, cosine, sine):
    return (normed * cosine + turn(normed) * sine).astype(BF16)


def row_blocks(length):
    step = min(length, 512)
    return [(at, step) for at in range(0, length, step)]


def forward_kernel(query_heads, key_heads, *refs):
    (projected, cosine_ref, sine_ref, column, row, query_gain, key_gain, attended, logs) = refs
    cosine, sine = cosine_ref[...], sine_ref[...]
    group = query_heads // key_heads
    scale = HEAD_SIZE ** (-0.5)
    length = projected.shape[0]
    for key_head in range(key_heads):
        key_hat, _ = normalized(head_columns(projected, query_heads + key_head))
        key = rotated(key_hat * key_gain[...], cosine, sine)
        value = head_columns(projected, query_heads + key_heads + key_head).astype(BF16)
        for head in range(key_head * group, (key_head + 1) * group):
            query_hat, _ = normalized(head_columns(projected, head))
            query = rotated(query_hat * query_gain[...], cosine, sine)
            for at, step in row_blocks(length):
                scores = rows_by_t(query[at : at + step], key) * scale
                allowed = row[...] <= column[at : at + step, :]
                scores = jnp.where(allowed, scores, MASK_FLOOR)
                peak = jnp.max(scores, axis=-1, keepdims=True)
                total = jnp.sum(jnp.exp(scores - peak), axis=-1, keepdims=True)
                log_total = peak + jnp.log(total)
                weights = jnp.exp(scores - log_total).astype(BF16)
                attended[at : at + step, head * HEAD_SIZE : (head + 1) * HEAD_SIZE] = rows_by(
                    weights, value
                ).astype(BF16)
                logs[at : at + step, head : head + 1] = log_total


def backward_kernel(query_heads, key_heads, *refs):
    (
        projected,
        cosine_ref,
        sine_ref,
        column,
        row,
        query_gain,
        key_gain,
        logs,
        attended,
        attended_grad,
        grad_projected,
        gain_parts,
    ) = refs
    cosine, sine = cosine_ref[...], sine_ref[...]
    group = query_heads // key_heads
    scale = HEAD_SIZE ** (-0.5)
    length = projected.shape[0]
    query_part = jnp.zeros((1, HEAD_SIZE), F32)
    key_part = jnp.zeros((1, HEAD_SIZE), F32)

    def finish(grad_rotary, hat, factor, gain):
        grad = grad_rotary * scale
        unrotated = grad * cosine - turn(grad) * sine
        part = jnp.sum(unrotated * hat, axis=0, keepdims=True)
        grad_hat = unrotated * gain
        inner = jnp.mean(grad_hat * hat, axis=-1, keepdims=True)
        return (factor * (grad_hat - hat * inner)).astype(BF16), part

    def store(head, values):
        grad_projected[:, head * HEAD_SIZE : (head + 1) * HEAD_SIZE] = values

    for key_head in range(key_heads):
        key_hat, key_scale = normalized(head_columns(projected, query_heads + key_head))
        key = rotated(key_hat * key_gain[...], cosine, sine)
        value = head_columns(projected, query_heads + key_heads + key_head).astype(BF16)
        key_acc = jnp.zeros((length, HEAD_SIZE), F32)
        value_acc = jnp.zeros((length, HEAD_SIZE), F32)
        for head in range(key_head * group, (key_head + 1) * group):
            query_hat, query_scale = normalized(head_columns(projected, head))
            query = rotated(query_hat * query_gain[...], cosine, sine)
            grad = head_columns(attended_grad, head)
            delta = jnp.sum(
                grad.astype(F32) * head_columns(attended, head).astype(F32), axis=-1, keepdims=True
            )
            query_accs = []
            for at, step in row_blocks(length):
                rows = slice(at, at + step)
                scores = rows_by_t(query[rows], key) * scale
                allowed = row[...] <= column[rows, :]
                scores = jnp.where(allowed, scores, MASK_FLOOR)
                probs = jnp.exp(scores - logs[rows, head : head + 1])
                grad_probs = rows_by_t(grad[rows], value)
                grad_scores = (probs * (grad_probs - delta[rows])).astype(BF16)
                query_accs.append(rows_by(grad_scores, key))
                key_acc = key_acc + t_by_rows(grad_scores, query[rows])
                value_acc = value_acc + t_by_rows(probs.astype(BF16), grad[rows])
            query_acc = jnp.concatenate(query_accs, axis=0)
            grads, part = finish(query_acc, query_hat, query_scale, query_gain[...])
            query_part = query_part + part
            store(head, grads)
        grads, part = finish(key_acc, key_hat, key_scale, key_gain[...])
        key_part = key_part + part
        store(query_heads + key_head, grads)
        store(query_heads + key_heads + key_head, value_acc.astype(BF16))
    gain_parts[0:1, :] = query_part
    gain_parts[1:2, :] = key_part


def attention_call(kernel, heads, operands, outs):
    whole = pl.BlockSpec(memory_space=pltpu.VMEM)
    return pl.pallas_call(
        lambda *refs: kernel(*heads, *refs),
        out_shape=outs,
        in_specs=[whole] * len(operands),
        out_specs=[whole] * len(outs),
    )(*operands)


def weight_grad_kernel(left, right, *refs):
    outs, turned = refs[:-1], refs[-1]

    @pl.when(pl.program_id(0) == 0)
    def _():
        turned[...] = left[...].T

    rows = outs[0].shape[0]
    for j, out in enumerate(outs):
        out[...] = rows_by(turned[j * rows : (j + 1) * rows], right[...]).astype(BF16)


def weight_grad(left, right, count=1):
    length, depth = left.shape
    width = right.shape[1]
    tile = HEAD_SIZE * 4 if width % (HEAD_SIZE * 4) == 0 else HEAD_SIZE
    return pl.pallas_call(
        weight_grad_kernel,
        grid=(width // tile,),
        out_shape=[jax.ShapeDtypeStruct((depth // count, width), BF16)] * count,
        in_specs=[
            pl.BlockSpec((length, depth), lambda j: (0, 0), pipeline_mode=pl.Buffered(1)),
            pl.BlockSpec((length, tile), lambda j: (0, j)),
        ],
        out_specs=[pl.BlockSpec((depth // count, tile), lambda j: (0, j))] * count,
        scratch_shapes=[pltpu.VMEM((depth, length), BF16)],
        name="weight_grad",
    )(left, right)


def weight_grad_sorted_kernel(cores, core, left, right, out, turned):
    rows = turned.shape[0] // cores

    @pl.when(pl.program_id(0) == 0)
    def _():
        for j in range(cores):
            at = pl.multiple_of((core[0] ^ j) * rows, rows)
            turned[pl.ds(at, rows)] = left[:, j * rows : (j + 1) * rows].T

    out[...] = rows_by(turned[...], right[...]).astype(BF16)


def weight_grad_sorted(left, right):
    cores = lax.axis_size("fsdp")
    length, depth = left.shape
    width = right.shape[1]
    tile = HEAD_SIZE * 4 if width % (HEAD_SIZE * 4) == 0 else HEAD_SIZE
    return pl.pallas_call(
        lambda *refs: weight_grad_sorted_kernel(cores, *refs),
        grid=(width // tile,),
        out_shape=jax.ShapeDtypeStruct((depth, width), BF16),
        in_specs=[
            pl.BlockSpec(memory_space=pltpu.SMEM),
            pl.BlockSpec((length, depth), lambda t: (0, 0), pipeline_mode=pl.Buffered(1)),
            pl.BlockSpec((length, tile), lambda t: (0, t)),
        ],
        out_specs=pl.BlockSpec((depth, tile), lambda t: (0, t)),
        scratch_shapes=[pltpu.VMEM((depth, length), BF16)],
        name="weight_grad",
    )(lax.axis_index("fsdp").astype(jnp.int32)[None], left, right)


def local(
    inputs,
    block_index,
    attention_gain,
    query_norm_gain,
    key_gain,
    feedforward_gain,
    attention_in,
    attention_out,
    gate_up,
    down_weight,
    grad_output,
):
    parts, cores = lax.axis_size("ctx"), lax.axis_size("fsdp")
    me = lax.axis_index("ctx")
    tokens = inputs.shape[1]
    half_rows = tokens // 2
    length = tokens * parts
    query_heads = QUERY_HEADS // parts
    key_heads = max(1, KEY_VALUE_HEADS // parts)
    copies = key_heads * parts // KEY_VALUE_HEADS
    query_width = query_heads * HEAD_SIZE
    key_width = key_heads * HEAD_SIZE
    all_query = QUERY_HEADS * HEAD_SIZE
    all_key = KEY_VALUE_HEADS * HEAD_SIZE
    hidden_width = FF // parts

    in_width = query_width + 2 * key_width
    own_key = (me // copies) * key_width
    own_inputs = to_relative(inputs[0])
    sequence_inputs = gather_ctx(own_inputs)
    blocks = gather_ctx(block_index[0]).reshape(-1)
    own_grad = to_relative(grad_output[0])
    sequence_grad = gather_ctx(own_grad)
    first_gain, second_gain = (
        to_relative(gain[None])[0] for gain in (attention_gain, feedforward_gain)
    )

    picked_in = pick_columns(
        [attention_in],
        [
            (0, me * query_width, query_width),
            (0, all_query + own_key, key_width),
            (0, all_query + all_key + own_key, key_width),
        ],
    )
    (weight_in,) = gather_plane(*picked_in, [in_width])
    picked_out = pick_columns(
        [attention_out], [(0, (me ^ j) * query_width, query_width) for j in range(parts)]
    )
    (weight_out,) = gather_plane(*picked_out, [all_query])
    picked_ff = pick_columns(
        [gate_up, down_weight],
        [
            (0, me * hidden_width, hidden_width),
            (0, FF + me * hidden_width, hidden_width),
            (1, me * hidden_width, hidden_width),
        ],
    )
    weight_gate_up, weight_down = gather_plane(*picked_ff, [2 * hidden_width, hidden_width], True)

    steps_along = jnp.arange(half_rows, dtype=jnp.int32)
    positions = (blocks[:, None] * half_rows + steps_along[None, :]).reshape(-1)
    cosine_table, sine_table = rope_tables(positions)

    rows = sequence_inputs.astype(F32)
    first_scale = rms_scale(rows)
    first_hat = rows * first_scale
    first_normed = (first_hat * first_gain).astype(BF16)
    projected = times(first_normed, weight_in)
    heads = (query_heads, key_heads)
    shared = [
        projected,
        cosine_table,
        sine_table,
        positions[:, None],
        positions[None, :],
        query_norm_gain[None],
        key_gain[None],
    ]
    attended, logs = attention_call(
        forward_kernel,
        heads,
        shared,
        [
            jax.ShapeDtypeStruct((length, query_width), BF16),
            jax.ShapeDtypeStruct((length, query_heads), F32),
        ],
    )

    all_attended = gather_heads(attended)
    middle = rows + jnp.concatenate(times_t(all_attended, weight_out), axis=1)
    second_scale = rms_scale(middle)
    second_hat = middle * second_scale
    second_normed = (second_hat * second_gain).astype(BF16)
    own_middle, own_second_hat = middle[:tokens], second_hat[:tokens]
    own_second_scale = second_scale[:tokens]

    grad_hidden = times(sequence_grad, weight_down, True)
    gate_values = times(second_normed, weight_gate_up)
    gate = gate_values[:, :hidden_width]
    upward = gate_values[:, hidden_width:]
    sigmoid_gate = jax.nn.sigmoid(gate)
    silu_gate = gate * sigmoid_gate
    hidden = (silu_gate * upward).astype(BF16)
    grad_gate = grad_hidden * upward * sigmoid_gate * (1.0 + gate * (1.0 - sigmoid_gate))
    grad_upward = grad_hidden * silu_gate
    grad_gate_up = jnp.concatenate([grad_gate, grad_upward], axis=1).astype(BF16)
    grad_second = jnp.concatenate(
        [
            scatter_ctx_direct(lax.optimization_barrier(rows_by_t(grad_gate_up, weight)))
            for weight in weight_gate_up
        ],
        axis=1,
    )
    gate_up_weight_grad = weight_grad_sorted(second_normed, grad_gate_up)
    down_weight_grad = weight_grad(sequence_grad, hidden, cores)
    gate_up_pieces = scatter_weight(gate_up_weight_grad, scatter_plane)
    down_pieces = scatter_weight(down_weight_grad, scatter_halves)
    partial_output = times_t(hidden, weight_down)

    feedforward_part = jnp.sum(grad_second * own_second_hat, axis=0)
    grad_middle = own_grad.astype(F32) + rms_back(
        grad_second, own_second_hat, own_second_scale, second_gain
    )
    grad_middle_short = grad_middle.astype(BF16)
    own_attended_grad = times(grad_middle_short, weight_out).astype(BF16)
    attended_grad = tokens_to_heads(own_attended_grad)
    middle_grad_rows = tokens_to_rows(grad_middle_short)
    (out_weight_grad,) = weight_grad(middle_grad_rows, all_attended)
    out_weight_sum = scatter_plane_swaps(out_weight_grad)
    output_sum = scatter_ctx(partial_output)
    output = from_relative((own_middle + output_sum).astype(BF16))[None]
    grad_projected, gain_parts = attention_call(
        backward_kernel,
        heads,
        shared + [logs, attended, attended_grad],
        [
            jax.ShapeDtypeStruct((length, in_width), BF16),
            jax.ShapeDtypeStruct((2, HEAD_SIZE), F32),
        ],
    )
    partial_first = times_t(grad_projected, weight_in)
    depth = D // cores
    attention_part = jnp.concatenate(
        [
            jnp.sum(part * first_hat[:, j * depth : (j + 1) * depth], axis=0)
            for j, part in enumerate(partial_first)
        ]
    )
    grad_first = scatter_ctx(partial_first)
    in_weight_grad = weight_grad(first_normed, grad_projected, cores)
    in_pieces = scatter_weight(in_weight_grad, scatter_halves)
    source = (me * cores + lax.axis_index("fsdp")) % parts
    (attention_in_grad,) = join_pieces(
        source,
        in_pieces,
        [
            [
                (0, query_width, 0, 1),
                (query_width, key_width, all_query, copies),
                (query_width + key_width, key_width, all_query + all_key, copies),
            ]
        ],
    )
    out_pieces = [
        out_weight_sum[:, j * query_width : (j + 1) * query_width] for j in range(parts)
    ]
    (attention_out_grad,) = join_pieces(
        me, out_pieces, [[(0, query_width, 0, 1)]])
    (gate_up_grad,) = join_pieces(
        source,
        gate_up_pieces, [[(0, hidden_width, 0, 1), (hidden_width, hidden_width, FF, 1)]]
    )
    (down_grad,) = join_pieces(
        source, down_pieces, [[(0, hidden_width, 0, 1)]])
    input_grad = grad_middle + rms_back(
        grad_first, first_hat[:tokens], first_scale[:tokens], first_gain
    )
    input_grad = from_relative(input_grad.astype(BF16))[None]
    gains = sum_everywhere(
        jnp.concatenate(
            [
                from_relative(attention_part[None])[0],
                gain_parts.reshape(-1),
                from_relative(feedforward_part[None])[0],
            ]
        ),
    )
    marks = [D, D + HEAD_SIZE, D + 2 * HEAD_SIZE]
    gain_sums = jnp.split(gains, marks)

    return (
        output,
        input_grad,
        gain_sums[0],
        gain_sums[1],
        gain_sums[2],
        gain_sums[3],
        attention_in_grad,
        attention_out_grad,
        gate_up_grad,
        down_grad,
    )


def solution(mesh):
    tokens = P(("seq", "fsdp"), "ctx", None)
    weight = P(("seq", "fsdp"), None)
    grad = P(("seq", "ctx", "fsdp"), None)
    in_specs = (tokens, tokens, P(), P(), P(), P(), weight, weight, weight, weight, tokens)
    out_specs = (tokens, tokens, P(), P(), P(), P(), grad, grad, grad, grad)
    return jax.shard_map(local, mesh=mesh, in_specs=in_specs, out_specs=out_specs, check_vma=False)
```
